512 devices in a mesh: tok: 64 (over z, y), head: 8 (over x, core).
Axes of the slice: x: 4, y: 4, z: 16, core: 2. Of those that a mesh axis runs over, the one named last changes fastest.
Arguments:
- inputs: bfloat16 [2, 16384, 2048], P(None, 'tok', 'head'), may hold values from -6 to 6
- probe_projector: bfloat16 [2048, 2048], P(None, 'head'), may hold values from -0.125 to 0.125
- address_projector: bfloat16 [2048, 2048], P(None, 'head'), may hold values from -0.125 to 0.125
- payload_projector: bfloat16 [2048, 2048], P(None, 'head'), may hold values from -0.125 to 0.125
- checkpoints: bfloat16 [2, 3, 8, 256, 512], P(None, None, 'head', 'tok'), may hold values from -0.375 to 0.375
- out_grad: bfloat16 [2, 16384, 2048], P(None, 'tok', 'head'), may hold values from -16 to 16
- adjoint: float32 [3, 8, 256, 512], P(None, 'head', 'tok'), may hold values from -96 to 96
- inner_rate: float32 [8], P('head'), may hold values from 0.25 to 4
Outputs:
- input_grad: bfloat16 [2, 16384, 2048], P(None, 'tok', 'head')
The draws below stay inside these ranges and needn't reach their ends.
All inputs are finite; a program needn't handle non-finite values.
Results may differ from the reference program's by a relative error of at most 0.014.
Values may be sent and summed in bfloat16 or wider, within the bound.
A program may use at most 64 MiB of HBM per device.

```python
import math
import jax
import jax.numpy as jnp
from jax import lax

D = 2048
H = 8
DH = 256
F = 512
STEPS = 2
TOKENS = 16384
N_HEAD = 8


def with_spikes(values, own_key, source, target, shards_of, factor):
    owner, partner = [(jnp.arange(values.shape[position]) // (values.shape[position] // shards_of)).reshape([-1 if axis == position else 1 for axis in range(values.ndim)]) for position in (source, target)]
    chosen = jax.random.permutation(own_key, shards_of)[partner]
    strong = (owner == chosen) | (owner == (partner + shards_of // 2) % shards_of)
    return jnp.where(strong, factor * values, values)


def steps_of(own_key, shape, shards, low, high):
    def one(position, parts):
        steps = jax.random.uniform(jax.random.fold_in(jax.random.fold_in(own_key, 6), position), (parts,), jnp.float32, low / len(shards), high / len(shards))
        return jnp.repeat(jnp.exp(steps), shape[position] // parts).reshape((-1,) + (1,) * (len(shape) - position - 1))

    gain = one(*shards[0])
    for cut in shards[1:]:
        gain = gain * one(*cut)
    return gain


def scatter_about(stream_key, dims, deviation, most, shards=(), kind=jnp.bfloat16):
    array = deviation * jax.random.normal(stream_key, dims, jnp.float32)
    if shards:
        array = array * steps_of(stream_key, dims, shards, -0.22, 0.18)
    return jnp.clip(array, -most, most).astype(kind)


def heavy_noise(own_key, dims, spread, bound, pieces, heavy, kind=jnp.bfloat16):
    entries = spread * jax.random.normal(own_key, dims, jnp.float32)
    if pieces:
        entries = entries * steps_of(own_key, dims, pieces, -0.22, 0.18)
    return jnp.clip(with_spikes(entries, jax.random.fold_in(own_key, 3), *heavy), -bound, bound).astype(kind)


def setup_inputs(seed: int = 0) -> dict:
    keys = jax.random.split(jax.random.key(seed), 9)
    inputs = scatter_about(keys[0], (STEPS, TOKENS, D), 1.0, 6.0, ((1, 64), (2, 8)))
    probe_projector = scatter_about(keys[1], (D, D), D ** -0.5, 0.125, ((1, 8),))
    address_projector = scatter_about(keys[2], (D, D), D ** -0.5, 0.125, ((1, 8),))
    payload_projector = scatter_about(keys[3], (D, D), D ** -0.5, 0.125, ((1, 8),))
    checkpoints = scatter_about(keys[4], (STEPS, 3, H, DH, F), DH ** -0.5, 0.375, ((2, 8), (3, 64)))
    out_grad = heavy_noise(keys[5], (STEPS, TOKENS, D), 1.0, 16.0, ((1, 64), (2, 8)), (1, 2, 64, 4.0))
    adjoint = scatter_about(keys[6], (3, H, DH, F), 16.0, 96.0, ((1, 8), (2, 64)), jnp.float32)
    inner_rate = jnp.clip(jnp.exp(math.log(4.0) - 2.7725887 * jax.random.uniform(keys[7], (H,), jnp.float32) ** steps_of(keys[7], (H,), ((0, 8),), -0.2, 0.2)), 0.25, 4.0)
    return dict(inputs=inputs, probe_projector=probe_projector, address_projector=address_projector, payload_projector=payload_projector, checkpoints=checkpoints, out_grad=out_grad, adjoint=adjoint, inner_rate=inner_rate)


def silu_terms(preact):
    sigma = jax.nn.sigmoid(preact)
    slope = sigma * (1.0 + preact * (1.0 - sigma))
    curvature = sigma * (1.0 - sigma) * (2.0 + preact * (1.0 - 2.0 * sigma))
    return preact * sigma, slope, curvature


def batched(form, left, right):
    return jnp.einsum(form, left.astype(jnp.float32), right.astype(jnp.float32))


def reference(inputs, probe_projector, address_projector, payload_projector, checkpoints, out_grad, adjoint, inner_rate):
    tokens = inputs.shape[1]
    projection = jnp.concatenate([probe_projector, address_projector, payload_projector], axis=1)
    blocked = projection.reshape(D, 3, H, DH)
    factor = (inner_rate / tokens)[None, :, None]
    adjoint_now = adjoint
    results = []
    per_group = H // N_HEAD
    for span in reversed(range(STEPS)):
        projected = jnp.dot(inputs[span], projection, preferred_element_type=jnp.float32).astype(jnp.bfloat16)
        projected = projected.reshape(tokens, 3, H, DH)
        queries = projected[:, 0]
        keys_now = projected[:, 1]
        values = projected[:, 2]
        grad_now = out_grad[span].reshape(tokens, H, DH)
        first_weight = checkpoints[span, 0]
        third_weight = checkpoints[span, 1]
        second_weight = checkpoints[span, 2]
        adjoint_bf = adjoint_now.astype(jnp.bfloat16)
        ahead = "nhd,hdf->nhf"
        gate_query = batched(ahead, queries, first_weight)
        lift_query = batched(ahead, queries, third_weight)
        back_query = batched(ahead, grad_now, second_weight)
        gate_keys = batched(ahead, keys_now, first_weight)
        lift_keys = batched(ahead, keys_now, third_weight)
        echo_values = batched(ahead, values, second_weight)
        pull_values = batched(ahead, values, adjoint_bf[2])
        side_one = batched(ahead, keys_now, adjoint_bf[0])
        side_three = batched(ahead, keys_now, adjoint_bf[1])
        swish_query, slope_query, unused = silu_terms(gate_query)
        swish_keys, slope_keys, bend_keys = silu_terms(gate_keys)
        hidden_act = (swish_query * lift_query).astype(jnp.bfloat16)
        gate_back = (back_query * lift_query * slope_query).astype(jnp.bfloat16)
        lift_back = (back_query * swish_query).astype(jnp.bfloat16)
        gate_second = (factor * (slope_keys * lift_keys * pull_values + side_one * echo_values * lift_keys * bend_keys + side_three * echo_values * slope_keys)).astype(jnp.bfloat16)
        lift_second = (factor * (swish_keys * pull_values + side_one * echo_values * slope_keys)).astype(jnp.bfloat16)
        down_second = (factor * (side_one * lift_keys * slope_keys + side_three * swish_keys)).astype(jnp.bfloat16)
        pull_second = (factor * swish_keys * lift_keys).astype(jnp.bfloat16)
        side_first = (factor * echo_values * lift_keys * slope_keys).astype(jnp.bfloat16)
        side_third = (factor * echo_values * swish_keys).astype(jnp.bfloat16)
        if span > 0:
            outer = "nhd,nhf->hdf"
            adjoint_now = adjoint_now + jnp.stack([
                batched(outer, keys_now, gate_second) + batched(outer, queries, gate_back),
                batched(outer, keys_now, lift_second) + batched(outer, queries, lift_back),
                batched(outer, values, down_second) + batched(outer, grad_now, hidden_act)])
        behind = "nhf,hdf->nhd"
        query_grad = (batched(behind, gate_back, first_weight) + batched(behind, lift_back, third_weight)).astype(jnp.bfloat16)
        keys_grad = (batched(behind, gate_second, first_weight) + batched(behind, lift_second, third_weight)
                     + batched(behind, side_first, adjoint_bf[0]) + batched(behind, side_third, adjoint_bf[1])).astype(jnp.bfloat16)
        values_grad = (batched(behind, down_second, second_weight) + batched(behind, pull_second, adjoint_bf[2])).astype(jnp.bfloat16)
        grads = jnp.stack([query_grad, keys_grad, values_grad], axis=1)
        running = jnp.zeros((tokens, D), jnp.float32)
        for group_index in range(N_HEAD):
            lower = group_index * per_group
            group_grad = grads[:, :, lower:lower + per_group].reshape(tokens, 3 * per_group * DH)
            group_weight = blocked[:, :, lower:lower + per_group].reshape(D, 3 * per_group * DH)
            partial_value = lax.dot_general(group_grad, group_weight, (((1,), (1,)), ((), ())), preferred_element_type=jnp.float32)
            rounded = lax.optimization_barrier(partial_value.astype(jnp.bfloat16))
            running = running + rounded.astype(jnp.float32)
        results.append(running.astype(jnp.bfloat16))
    return jnp.stack(results[::-1])
```

```python
import jax
import jax.numpy as jnp
from jax import lax
from jax.experimental import pallas as pl
from jax.experimental.pallas import tpu as pltpu
from jax.sharding import Mesh
from jax.sharding import PartitionSpec as P

AXES = ("z", "y", "x", "c")
NZ, NY, NX, NC = 16, 4, 4, 2
MESH = pl.DeviceIdType.MESH
BF = jnp.bfloat16
F32 = jnp.float32
T = 256
DH = 256
F = 512
D = 2048
W_LATE, B_LATE, W_EARLY, B_EARLY = 0, 1, 2, 3


def mm(a, b):
    return jnp.dot(a, b, preferred_element_type=F32)


def mm_t(a, b):
    return lax.dot_general(a, b, (((1,), (1,)), ((), ())), preferred_element_type=F32)


def t_mm(a, b):
    return lax.dot_general(a, b, (((0,), (0,)), ((), ())), preferred_element_type=F32)


def native_row(position, near_first):
    high, middle = position // 64, (position // 16) % 4
    y, low = (middle, high) if near_first else (high, middle)
    return 64 * ((position // 4) % 4) + 16 * low + 4 * y + position % 4


def permutation(near_first):
    row = lax.broadcasted_iota(jnp.int32, (DH, DH), 0)
    position = lax.broadcasted_iota(jnp.int32, (DH, DH), 1)
    return jnp.where(row == native_row(position, near_first), 1.0, 0.0).astype(BF)


def kernel(
    xin, pq, pk, pv, ck, og, adj, rate, out,
    xg, pc, pp, gath, fb, tile, qkv, o_s, fw, hb, own, rsend,
    ry, acc1, s1, rn, rn2, acc2, s2, ry2, fs, fsf, rf, gcat, gp, pb, ro,
    xs, xr, fas, far, nas, nar, yas, yar, nbs, nbr, ybs, ybr,
    rys, ryr, rns, rnr, rn2s, rn2r, ry2s, ry2r, rfs, rfr, cs, cr, hs, hr,
):
    z, y = lax.axis_index("z"), lax.axis_index("y")
    x, c = lax.axis_index("x"), lax.axis_index("c")

    def dev(dz=0, dy=0, dx=0, dc=0):
        return (
            lax.rem(z + dz + NZ, NZ), lax.rem(y + dy, NY), lax.rem(x + dx, NX), lax.rem(c + dc, NC)
        )

    zh, zl = z // 4, lax.rem(z, 4)
    skip = 4 * c - 2
    near = [1, -1, skip]
    fars = [4, -4, 8]

    barrier = pltpu.get_barrier_semaphore()
    partners = [dev(dz=d) for d in (1, -1, 2, -2, 4, -4, 8)]
    partners += [dev(dy=d) for d in (1, 2, 3)] + [dev(dx=d) for d in (1, 2, 3)] + [dev(dc=1)]
    for partner in partners:
        pl.semaphore_signal(barrier, inc=1, device_id=partner, device_id_type=MESH)

    started = []

    def send(src, dst, ssem, rsem, device):
        copy = pltpu.make_async_remote_copy(
            src_ref=src, dst_ref=dst, send_sem=ssem, recv_sem=rsem,
            device_id=device, device_id_type=MESH,
        )
        copy.start()
        started.append(copy)
        return copy

    fb[W_LATE, zh] = ck[1]
    fb[W_EARLY, zh] = ck[0]
    fb[B_LATE, zh] = adj[...].astype(BF)
    column = pl.multiple_of((x * 2 + c) * DH, DH)
    for s in range(2):
        xg[s, :, pl.ds(column, DH)] = xin[s]

    pl.semaphore_wait(barrier, len(partners))

    far_copies = {}

    def far_send(s):
        far_copies[s] = [
            send(fb.at[s, zh], fb.at[s, zh], fas.at[s, i], far.at[s, i], dev(dz=d))
            for i, d in enumerate(fars)
        ]

    x_copies = {}

    def x_send(s):
        block = xg.at[s, :, pl.ds(column, DH)]
        x_copies[s] = [
            send(xin.at[s], block, xs.at[s, i], xr.at[s, i], dev(dx=i + 1)) for i in range(3)
        ]
        x_copies[s].append(send(xin.at[s], block, xs.at[s, 3], xr.at[s, 3], dev(dc=1)))

    far_send(W_LATE)
    far_send(B_LATE)
    x_send(1)
    x_send(0)
    far_send(W_EARLY)

    plain, swapped = permutation(False), permutation(True)
    for i, (ref, order) in enumerate(((pq, plain), (pk, plain), (pv, swapped))):
        for j in range(8):
            rows = pl.ds(j * DH, DH)
            pc[rows, pl.ds(i * DH, DH)] = mm(ref[rows, :], order).astype(BF)
    for s in range(2):
        o_s[s] = mm(og[s], swapped).astype(BF)

    other = 1 - c
    pc_copies = []
    for i in range(4):
        rows = pl.multiple_of((i * 2 + other) * DH, DH)
        pc_copies.append(
            send(pc.at[pl.ds(rows, DH), :], pp.at[i], cs.at[i], cr.at[i], dev(dc=1))
        )

    blocks01 = pl.multiple_of(y * 64 + zl * 16, 16)
    blocks2 = pl.multiple_of(zl * 64 + y * 16, 16)
    near_a, y_a, y_b, near_b = {}, {}, {}, {}

    def gather_far(s):
        for copy in far_copies[s]:
            copy.wait_recv()
        for m in range(3):
            for k in range(4):
                tile[m, pl.ds(4 * k, 4), :] = fb[s, k, m].astype(F32)
        gath[s, 0, pl.ds(blocks01, 16), :] = tile[0].astype(BF)
        gath[s, 1, pl.ds(blocks01, 16), :] = tile[1].astype(BF)
        gath[s, 2, pl.ds(blocks2, 16), :] = tile[2].astype(BF)
        first = gath.at[s, pl.ds(0, 2), pl.ds(blocks01, 16), :]
        second = gath.at[s, 2, pl.ds(blocks2, 16), :]
        near_a[s] = [
            send(first, first, nas.at[s, i], nar.at[s, i], dev(dz=d)) for i, d in enumerate(near)
        ]
        y_b[s] = [
            send(second, second, ybs.at[s, i], ybr.at[s, i], dev(dy=i + 1)) for i in range(3)
        ]

    def gather_middle(s):
        for copy in near_a[s]:
            copy.wait_recv()
        first = gath.at[s, pl.ds(0, 2), pl.ds(pl.multiple_of(y * 64, 64), 64), :]
        y_a[s] = [
            send(first, first, yas.at[s, i], yar.at[s, i], dev(dy=i + 1)) for i in range(3)
        ]
        for copy in y_b[s]:
            copy.wait_recv()
        second = gath.at[s, 2, pl.ds(pl.multiple_of(zl * 64, 64), 64), :]
        near_b[s] = [
            send(second, second, nbs.at[s, i], nbr.at[s, i], dev(dz=d)) for i, d in enumerate(near)
        ]

    def gather_end(s):
        for copy in y_a[s] + near_b[s]:
            copy.wait_recv()

    relays = {}

    def x_relay(s):
        relays[s] = []
        for i in range(3):
            x_copies[s][i].wait_recv()
            source = pl.multiple_of((lax.rem(x + 3 - i, NX) * 2 + c) * DH, DH)
            block = xg.at[s, :, pl.ds(source, DH)]
            relays[s].append(send(block, block, xs.at[s, 4 + i], xr.at[s, 4 + i], dev(dc=1)))

    def project(s):
        for copy in [x_copies[s][3]] + relays[s]:
            copy.wait_recv()
        for i in range(3):
            qkv[s, i] = mm(xg[s], pc[:, pl.ds(i * DH, DH)]).astype(BF)

    factor = rate[0] / 16384.0

    def forward(s, w):
        q, k, v = qkv[s, 0], qkv[s, 1], qkv[s, 2]
        fw[s, 0] = mm(q, gath[w, 0])
        fw[s, 1] = mm(q, gath[w, 1])
        fw[s, 2] = mm(o_s[s], gath[w, 2])
        fw[s, 3] = mm(k, gath[w, 0])
        fw[s, 4] = mm(k, gath[w, 1])
        fw[s, 5] = mm(v, gath[w, 2])

        @pl.loop(0, T // 16)
        def _(step):
            rows = pl.ds(pl.multiple_of(step * 16, 16), 16)
            gate, lift, back = fw[s, 0, rows, :], fw[s, 1, rows, :], fw[s, 2, rows, :]
            g = jax.nn.sigmoid(gate)
            act = gate * g
            if s > 0:
                hb[s, 0, rows, :] = (act * lift).astype(BF)
            hb[s, 1, rows, :] = (back * lift * (g * (1.0 + gate * (1.0 - g)))).astype(BF)
            hb[s, 2, rows, :] = (back * act).astype(BF)
            gate, u, e = fw[s, 3, rows, :], fw[s, 4, rows, :], fw[s, 5, rows, :]
            g = jax.nn.sigmoid(gate)
            act = factor * gate * g
            slope = factor * (g * (1.0 + gate * (1.0 - g)))
            bend = factor * (g * (1.0 - g) * (2.0 + gate * (1.0 - 2.0 * g)))
            us = u * slope
            fw[s, 0, rows, :] = us
            fw[s, 1, rows, :] = e * u * bend
            fw[s, 2, rows, :] = e * slope
            fw[s, 3, rows, :] = act
            hb[s, 6, rows, :] = (act * u).astype(BF)
            hb[s, 7, rows, :] = (e * us).astype(BF)
            hb[s, 8, rows, :] = (e * act).astype(BF)

    def second(s, b):
        fw[s, 6] = mm(qkv[s, 2], gath[b, 2])
        fw[s, 7] = mm(qkv[s, 1], gath[b, 0])
        fw[s, 8] = mm(qkv[s, 1], gath[b, 1])

        @pl.loop(0, T // 16)
        def _(step):
            rows = pl.ds(pl.multiple_of(step * 16, 16), 16)
            pull, one, three = fw[s, 6, rows, :], fw[s, 7, rows, :], fw[s, 8, rows, :]
            us, eub, es, act = (fw[s, i, rows, :] for i in range(4))
            hb[s, 3, rows, :] = (us * pull + one * eub + three * es).astype(BF)
            hb[s, 4, rows, :] = (act * pull + one * es).astype(BF)
            hb[s, 5, rows, :] = (one * us + three * act).astype(BF)

    def back_queries(s, w):
        grad = mm_t(hb[s, 1], gath[w, 0]) + mm_t(hb[s, 2], gath[w, 1])
        gcat[s, :, pl.ds(0, DH)] = grad.astype(BF)

    def back_rest(s, w, b):
        grad = mm_t(hb[s, 3], gath[w, 0]) + mm_t(hb[s, 4], gath[w, 1])
        grad = grad + mm_t(hb[s, 7], gath[b, 0]) + mm_t(hb[s, 8], gath[b, 1])
        gcat[s, :, pl.ds(DH, DH)] = grad.astype(BF)
        grad = mm_t(hb[s, 5], gath[w, 2]) + mm_t(hb[s, 6], gath[b, 2])
        gcat[s, :, pl.ds(2 * DH, DH)] = grad.astype(BF)

    pair = {}

    def exchange(s):
        pair[s] = send(gcat.at[s], gp.at[s], cs.at[4 + s], cr.at[4 + s], dev(dc=1))

    heads = {}

    def partial_of(s, step):
        to = lax.rem(x + step, NX)
        rows = pl.multiple_of((to * 2 + c) * DH, DH)
        return mm_t(gcat[s], pc[pl.ds(rows, DH), :]) + mm_t(gp[s], pp[to])

    def heads_send(s):
        if s == 1:
            for copy in pc_copies:
                copy.wait_recv()
        pair[s].wait_recv()
        heads[s] = []
        for i, step in enumerate((2, 1, 3)):
            pb[s, i] = partial_of(s, step).astype(BF)
            heads[s].append(
                send(pb.at[s, i], ro.at[s, i], hs.at[s, i], hr.at[s, i], dev(dx=step))
            )

    def heads_end(s):
        total = partial_of(s, 0)
        for i in range(3):
            heads[s][i].wait_recv()
            total = total + ro[s, i].astype(F32)
        out[s] = total.astype(BF)

    gather_far(W_LATE)
    gather_far(B_LATE)
    x_relay(1)
    gather_middle(W_LATE)
    gather_middle(B_LATE)
    gather_far(W_EARLY)
    project(1)
    gather_end(W_LATE)
    forward(1, W_LATE)
    gather_middle(W_EARLY)
    gather_end(B_LATE)
    second(1, B_LATE)

    q, k, v = qkv[1, 0], qkv[1, 1], qkv[1, 2]
    ry_copies = []
    for m in range(2):
        own[m] = t_mm(k, hb[1, 3 + m]) + t_mm(q, hb[1, 1 + m])
        rsend[m] = own[m].astype(BF)
        for i in range(3):
            rows = pl.multiple_of(lax.rem(y + i + 1, NY) * 64, 64)
            ry_copies.append(
                send(rsend.at[m, pl.ds(rows, 64), :], ry.at[m, i], rys.at[m, i], ryr.at[m, i],
                     dev(dy=i + 1))
            )
    own[2] = t_mm(v, hb[1, 5]) + t_mm(o_s[1], hb[1, 0])
    rsend[2] = own[2].astype(BF)
    rn2_copies = []
    for i, d in enumerate(near):
        rows = pl.multiple_of(lax.rem(z + d + NZ, 4) * 64, 64)
        rn2_copies.append(
            send(rsend.at[2, pl.ds(rows, 64), :], rn2.at[i], rn2s.at[i], rn2r.at[i], dev(dz=d))
        )

    back_queries(1, W_LATE)
    back_rest(1, W_LATE, B_LATE)
    exchange(1)

    for copy in rn2_copies:
        copy.wait_recv()
    total = own[2, pl.ds(pl.multiple_of(zl * 64, 64), 64), :]
    for i in range(3):
        total = total + rn2[i].astype(F32)
    acc2[...] = total
    s2[...] = total.astype(BF)
    ry2_copies = []
    for i in range(3):
        rows = pl.multiple_of(lax.rem(y + i + 1, NY) * 16, 16)
        ry2_copies.append(
            send(s2.at[pl.ds(rows, 16), :], ry2.at[i], ry2s.at[i], ry2r.at[i], dev(dy=i + 1))
        )
    for copy in ry_copies:
        copy.wait_recv()
    for m in range(2):
        total = own[m, pl.ds(pl.multiple_of(y * 64, 64), 64), :]
        for i in range(3):
            total = total + ry[m, i].astype(F32)
        acc1[m] = total
        s1[m] = total.astype(BF)
    rn_copies = []
    for i, d in enumerate(near):
        rows = pl.multiple_of(lax.rem(z + d + NZ, 4) * 16, 16)
        rn_copies.append(
            send(s1.at[:, pl.ds(rows, 16), :], rn.at[i], rns.at[i], rnr.at[i], dev(dz=d))
        )

    x_relay(0)
    gather_end(W_EARLY)
    project(0)

    for copy in ry2_copies + rn_copies:
        copy.wait_recv()
    for m in range(2):
        total = acc1[m, pl.ds(pl.multiple_of(zl * 16, 16), 16), :]
        for i in range(3):
            total = total + rn[i, m].astype(F32)
        tile[m] = total
    total = acc2[pl.ds(pl.multiple_of(y * 16, 16), 16), :]
    for i in range(3):
        total = total + ry2[i].astype(F32)
    tile[2] = total
    for m in range(3):
        for k4 in range(4):
            piece = tile[m, pl.ds(4 * k4, 4), :]
            fsf[k4, m] = piece
            fs[k4, m] = piece.astype(BF)
    rf_copies = []
    for i, d in enumerate(fars):
        to = lax.rem(z + d + NZ, NZ) // 4
        rf_copies.append(send(fs.at[to], rf.at[i], rfs.at[i], rfr.at[i], dev(dz=d)))

    forward(0, W_EARLY)

    for copy in rf_copies:
        copy.wait_recv()
    total = adj[...] + fsf[zh]
    for i in range(3):
        total = total + rf[i].astype(F32)
    fb[B_EARLY, zh] = total.astype(BF)
    far_send(B_EARLY)

    back_queries(0, W_EARLY)
    heads_send(1)

    gather_far(B_EARLY)
    heads_end(1)
    gather_middle(B_EARLY)
    gather_end(B_EARLY)

    second(0, B_EARLY)
    back_rest(0, W_EARLY, B_EARLY)
    exchange(0)
    heads_send(0)
    heads_end(0)

    for copy in started:
        copy.wait_send()


def local(inputs, probe, address, payload, checkpoints, out_grad, adjoint, inner_rate):
    vmem = pl.BlockSpec(memory_space=pltpu.VMEM)
    dma = pltpu.SemaphoreType.DMA
    scratch = [
        pltpu.VMEM((2, T, D), BF),
        pltpu.VMEM((D, 3 * DH), BF),
        pltpu.VMEM((4, DH, 3 * DH), BF),
        pltpu.VMEM((4, 3, DH, F), BF),
        pltpu.VMEM((4, 4, 3, 4, F), BF),
        pltpu.VMEM((3, 16, F), F32),
        pltpu.VMEM((2, 3, T, DH), BF),
        pltpu.VMEM((2, T, DH), BF),
        pltpu.VMEM((2, 9, T, F), F32),
        pltpu.VMEM((2, 9, T, F), BF),
        pltpu.VMEM((3, DH, F), F32),
        pltpu.VMEM((3, DH, F), BF),
        pltpu.VMEM((2, 3, 64, F), BF),
        pltpu.VMEM((2, 64, F), F32),
        pltpu.VMEM((2, 64, F), BF),
        pltpu.VMEM((3, 2, 16, F), BF),
        pltpu.VMEM((3, 64, F), BF),
        pltpu.VMEM((64, F), F32),
        pltpu.VMEM((64, F), BF),
        pltpu.VMEM((3, 16, F), BF),
        pltpu.VMEM((4, 3, 4, F), BF),
        pltpu.VMEM((4, 3, 4, F), F32),
        pltpu.VMEM((3, 3, 4, F), BF),
        pltpu.VMEM((2, T, 3 * DH), BF),
        pltpu.VMEM((2, T, 3 * DH), BF),
        pltpu.VMEM((2, 3, T, DH), BF),
        pltpu.VMEM((2, 3, T, DH), BF),
    ]
    for shape in ((2, 7), (4, 3), (4, 3), (4, 3), (4, 3), (4, 3), (2, 3), (3,), (3,), (3,), (3,), (6,), (2, 3)):
        scratch += [dma(shape), dma(shape)]
    return pl.pallas_call(
        kernel,
        name="meta_gradient",
        out_shape=jax.ShapeDtypeStruct((2, T, DH), BF),
        in_specs=[vmem] * 7 + [pl.BlockSpec(memory_space=pltpu.SMEM)],
        out_specs=vmem,
        scratch_shapes=scratch,
        compiler_params=pltpu.CompilerParams(
            collective_id=0, has_side_effects=True, vmem_limit_bytes=60 * 2**20
        ),
    )(
        inputs,
        probe,
        address,
        payload,
        checkpoints.reshape(2, 3, 4, F),
        out_grad,
        adjoint.reshape(3, 4, F),
        inner_rate,
    )


def solution(mesh):
    split = Mesh(mesh.devices.reshape(NZ, NY, NX, NC), AXES)
    tok, head = ("z", "y"), ("x", "c")
    placed = (
        P(None, tok, head),
        P(None, head),
        P(None, head),
        P(None, head),
        P(None, None, head, tok, None),
        P(None, tok, head),
        P(None, head, tok, None),
        P(head),
    )
    return jax.shard_map(
        local, mesh=split, in_specs=placed, out_specs=P(None, tok, head), check_vma=False
    )
```

```python
import jax
import jax.numpy as jnp
from jax import lax
from jax.experimental import pallas as pl
from jax.experimental.pallas import tpu as pltpu
from jax.sharding import Mesh
from jax.sharding import PartitionSpec as P

AXES = ("z", "y", "x", "c")
NZ, NY, NX, NC = 16, 4, 4, 2
MESH = pl.DeviceIdType.MESH
BF = jnp.bfloat16
F32 = jnp.float32
T = 256
DH = 256
F = 512
D = 2048
W_LATE, B_LATE, W_EARLY, B_EARLY = 0, 1, 2, 3


def mm(a, b):
    return jnp.dot(a, b, preferred_element_type=F32)


def mm_t(a, b):
    return lax.dot_general(a, b, (((1,), (1,)), ((), ())), preferred_element_type=F32)


def t_mm(a, b):
    return lax.dot_general(a, b, (((0,), (0,)), ((), ())), preferred_element_type=F32)


def permutation():
    row = lax.broadcasted_iota(jnp.int32, (DH, DH), 0)
    place = lax.broadcasted_iota(jnp.int32, (DH, DH), 1)
    held = 64 * ((place // 4) % 4) + 16 * ((place // 16) % 4) + 4 * (place // 64) + place % 4
    return jnp.where(row == held, 1.0, 0.0).astype(BF)


def kernel(
    xin, pq, pk, pv, ck, og, adj, rate, out,
    xg, pr, pc, pp, gath, fb, adjv, tile, ogv, qkv, o_s, fw, hb, own, rsend,
    r1, acc, sd, r2, part, fsend, rf, gcat, gp, pb, ro,
    ls, xs, xr, fs, fr, as_, ar, bs, br, r1s, r1r, r2s, r2r, rfs, rfr, cs, cr, hs, hr,
):
    z, y = lax.axis_index("z"), lax.axis_index("y")
    x, c = lax.axis_index("x"), lax.axis_index("c")

    def dev(dz=0, dy=0, dx=0, dc=0):
        return (
            lax.rem(z + dz + NZ, NZ), lax.rem(y + dy, NY), lax.rem(x + dx, NX), lax.rem(c + dc, NC)
        )

    zh, zl = z // 4, lax.rem(z, 4)
    skip = 4 * c - 2
    near = [1, -1, skip]

    barrier = pltpu.get_barrier_semaphore()
    partners = [dev(dz=d) for d in (4, -4, 2, -2, 1, -1)]
    partners += [dev(dy=d) for d in (1, 2, 3)] + [dev(dx=d) for d in (1, 2, 3)] + [dev(dc=1)]
    for partner in partners:
        pl.semaphore_signal(barrier, inc=1, device_id=partner, device_id_type=MESH)

    started = []

    def send(src, dst, ssem, rsem, device):
        copy = pltpu.make_async_remote_copy(
            src_ref=src, dst_ref=dst, send_sem=ssem, recv_sem=rsem,
            device_id=device, device_id_type=MESH,
        )
        copy.start()
        started.append(copy)
        return copy

    column = pl.multiple_of((x * 2 + c) * DH, DH)
    loads = [
        pltpu.make_async_copy(src, dst, ls.at[i])
        for i, (src, dst) in enumerate((
            (ck.at[1], fb.at[W_LATE, zh]),
            (adj, adjv),
            (ck.at[0], fb.at[W_EARLY, zh]),
            (xin.at[1], xg.at[1, :, pl.ds(column, DH)]),
            (pq, pr.at[0]),
            (pk, pr.at[1]),
            (pv, pr.at[2]),
            (og, ogv),
            (xin.at[0], xg.at[0, :, pl.ds(column, DH)]),
        ))
    ]
    for load in loads:
        load.start()
    for load in loads[:4]:
        load.wait()
    fb[B_LATE, zh] = adjv[...].astype(BF)

    pl.semaphore_wait(barrier, len(partners))

    far_copies = {}

    def far_send(i, sets):
        piece = fb.at[sets, zh]
        far_copies[i] = [
            send(piece, piece, fs.at[i, n], fr.at[i, n], dev(dz=d)) for n, d in enumerate((4, -4))
        ]

    def far_relay(i, sets):
        for copy in far_copies[i]:
            copy.wait_recv()
        below = fb.at[sets, lax.rem(zh + 3, 4), pl.ds(0, 1)]
        above = fb.at[sets, lax.rem(zh + 1, 4), pl.ds(1, 2)]
        far_copies[i] = [
            send(below, below, fs.at[i, 2], fr.at[i, 2], dev(dz=4)),
            send(above, above, fs.at[i, 3], fr.at[i, 3], dev(dz=-4)),
        ]

    x_copies = {}

    def x_send(s):
        block = xg.at[s, :, pl.ds(column, DH)]
        x_copies[s] = [
            send(xin.at[s], block, xs.at[s, i], xr.at[s, i], dev(dx=d)) for i, d in enumerate((2, 1, 3))
        ]
        x_copies[s].append(send(xin.at[s], block, xs.at[s, 3], xr.at[s, 3], dev(dc=1)))

    late, early = pl.ds(0, 2), pl.ds(2, 1)
    far_send(0, late)
    x_send(1)
    far_send(1, early)
    x_send(0)

    order = permutation()
    for i in range(3):
        loads[4 + i].wait()
        for j in range(8):
            rows = pl.ds(j * DH, DH)
            pc[rows, pl.ds(i * DH, DH)] = mm(pr[i, rows, :], order).astype(BF)

    far_relay(0, late)
    far_relay(1, early)

    other = 1 - c
    pc_copies = []
    for i in range(4):
        rows = pl.multiple_of((i * 2 + other) * DH, DH)
        pc_copies.append(
            send(pc.at[pl.ds(rows, DH), :], pp.at[i], cs.at[i], cr.at[i], dev(dc=1))
        )
    loads[7].wait()
    for s in range(2):
        o_s[s] = mm(ogv[s], order).astype(BF)

    first, last = {}, {}

    def to_near(block, ssem, rsem):
        return [send(block, block, ssem.at[i], rsem.at[i], dev(dz=d)) for i, d in enumerate(near)]

    def to_y(block, ssem, rsem):
        return [send(block, block, ssem.at[i], rsem.at[i], dev(dy=d)) for i, d in enumerate((2, 1, 3))]

    def swapped(s, half):
        return half == 1 and s != W_EARLY

    def gather_first(s):
        first[s] = []
        for half in range(2):
            block = gath.at[s, half, :, y, zl]
            stage = to_y if swapped(s, half) else to_near
            first[s] += stage(block, as_.at[s, half], ar.at[s, half])

    def gather_last(s):
        for copy in first[s]:
            copy.wait_recv()
        last[s] = []
        for half in range(2):
            if swapped(s, half):
                last[s] += to_near(gath.at[s, half, :, :, zl], bs.at[s, half], br.at[s, half])
            else:
                last[s] += to_y(gath.at[s, half, :, y], bs.at[s, half], br.at[s, half])

    def gather_end(s):
        for copy in last[s]:
            copy.wait_recv()

    def far_end(i):
        for copy in far_copies[i]:
            copy.wait_recv()

    def assemble(s):
        for m in range(3):
            for k in range(4):
                tile[m, pl.ds(4 * k, 4), :] = fb[s, k, m].astype(F32)
            gath[s, 0, m, y, zl] = tile[m, :, pl.ds(0, 256)].astype(BF)
            gath[s, 1, m, y, zl] = tile[m, :, pl.ds(256, 256)].astype(BF)

    relays = {}

    def x_relay(s):
        relays[s] = []
        for i, d in enumerate((2, 1, 3)):
            x_copies[s][i].wait_recv()
            source = pl.multiple_of((lax.rem(x + 4 - d, NX) * 2 + c) * DH, DH)
            block = xg.at[s, :, pl.ds(source, DH)]
            relays[s].append(send(block, block, xs.at[s, 4 + i], xr.at[s, 4 + i], dev(dc=1)))

    def project(s):
        for copy in [x_copies[s][3]] + relays[s]:
            copy.wait_recv()
        for i in range(3):
            qkv[s, i] = mm(xg[s], pc[:, pl.ds(i * DH, DH)]).astype(BF)

    factor = rate[0] / 16384.0

    def weight(s, half, m):
        return gath[s, half, m].reshape(DH, 256)

    def ahead(rows, s, m, to):
        for half in range(2):
            fw[to[0], to[1], :, pl.ds(half * 256, 256)] = mm(rows, weight(s, half, m))

    def behind(s, i, w, m):
        return mm_t(hb[s, i, :, pl.ds(0, 256)], weight(w, 0, m)) + mm_t(
            hb[s, i, :, pl.ds(256, 256)], weight(w, 1, m)
        )

    def forward(s, w):
        q, k, v = qkv[s, 0], qkv[s, 1], qkv[s, 2]
        ahead(q, w, 0, (s, 0))
        ahead(q, w, 1, (s, 1))
        ahead(o_s[s], w, 2, (s, 2))
        ahead(k, w, 0, (s, 3))
        ahead(k, w, 1, (s, 4))
        ahead(v, w, 2, (s, 5))

        @pl.loop(0, T // 16)
        def _(step):
            rows = pl.ds(pl.multiple_of(step * 16, 16), 16)
            gate, lift, back = fw[s, 0, rows, :], fw[s, 1, rows, :], fw[s, 2, rows, :]
            g = jax.nn.sigmoid(gate)
            act = gate * g
            if s > 0:
                hb[s, 0, rows, :] = (act * lift).astype(BF)
            hb[s, 1, rows, :] = (back * lift * (g * (1.0 + gate * (1.0 - g)))).astype(BF)
            hb[s, 2, rows, :] = (back * act).astype(BF)
            gate, u, e = fw[s, 3, rows, :], fw[s, 4, rows, :], fw[s, 5, rows, :]
            g = jax.nn.sigmoid(gate)
            act = factor * gate * g
            slope = factor * (g * (1.0 + gate * (1.0 - g)))
            bend = factor * (g * (1.0 - g) * (2.0 + gate * (1.0 - 2.0 * g)))
            us = u * slope
            fw[s, 0, rows, :] = us
            fw[s, 1, rows, :] = e * u * bend
            fw[s, 2, rows, :] = e * slope
            fw[s, 3, rows, :] = act
            hb[s, 6, rows, :] = (act * u).astype(BF)
            hb[s, 7, rows, :] = (e * us).astype(BF)
            hb[s, 8, rows, :] = (e * act).astype(BF)

    def second(s, b):
        ahead(qkv[s, 2], b, 2, (s, 6))
        ahead(qkv[s, 1], b, 0, (s, 7))
        ahead(qkv[s, 1], b, 1, (s, 8))

        @pl.loop(0, T // 16)
        def _(step):
            rows = pl.ds(pl.multiple_of(step * 16, 16), 16)
            pull, one, three = fw[s, 6, rows, :], fw[s, 7, rows, :], fw[s, 8, rows, :]
            us, eub, es, act = (fw[s, i, rows, :] for i in range(4))
            hb[s, 3, rows, :] = (us * pull + one * eub + three * es).astype(BF)
            hb[s, 4, rows, :] = (act * pull + one * es).astype(BF)
            hb[s, 5, rows, :] = (one * us + three * act).astype(BF)

    def back_queries(s, w):
        grad = behind(s, 1, w, 0) + behind(s, 2, w, 1)
        gcat[s, :, pl.ds(0, DH)] = grad.astype(BF)

    def back_rest(s, w, b):
        grad = behind(s, 3, w, 0) + behind(s, 4, w, 1)
        grad = grad + behind(s, 7, b, 0) + behind(s, 8, b, 1)
        gcat[s, :, pl.ds(DH, DH)] = grad.astype(BF)
        grad = behind(s, 5, w, 2) + behind(s, 6, b, 2)
        gcat[s, :, pl.ds(2 * DH, DH)] = grad.astype(BF)

    pair = {}

    def exchange(s):
        pair[s] = send(gcat.at[s], gp.at[s], cs.at[4 + s], cr.at[4 + s], dev(dc=1))

    heads = {}

    def partial_of(s, step):
        to = lax.rem(x + step, NX)
        rows = pl.multiple_of((to * 2 + c) * DH, DH)
        return mm_t(gcat[s], pc[pl.ds(rows, DH), :]) + mm_t(gp[s], pp[to])

    def heads_send(s):
        if s == 1:
            for copy in pc_copies:
                copy.wait_recv()
        pair[s].wait_recv()
        heads[s] = []
        for i, step in enumerate((2, 1, 3)):
            pb[s, i] = partial_of(s, step).astype(BF)
            heads[s].append(
                send(pb.at[s, i], ro.at[s, i], hs.at[s, i], hr.at[s, i], dev(dx=step))
            )

    def heads_end(s):
        total = partial_of(s, 0)
        for i in range(3):
            heads[s][i].wait_recv()
            total = total + ro[s, i].astype(F32)
        out[s] = total.astype(BF)

    far_end(0)
    assemble(W_LATE)
    gather_first(W_LATE)
    assemble(B_LATE)
    gather_first(B_LATE)
    gather_last(W_LATE)
    gather_last(B_LATE)
    x_relay(1)
    far_end(1)
    assemble(W_EARLY)
    gather_first(W_EARLY)
    project(1)
    gather_end(W_LATE)
    forward(1, W_LATE)
    gather_end(B_LATE)
    second(1, B_LATE)

    terms = (
        (qkv[1, 1], 3, qkv[1, 0], 1),
        (qkv[1, 1], 4, qkv[1, 0], 2),
        (qkv[1, 2], 5, o_s[1], 0),
    )
    sum_a, sum_b = {}, {}
    for m, (left, i, right, j) in enumerate(terms):
        for half in range(2):
            lanes = pl.ds(half * 256, 256)
            grad = t_mm(left, hb[1, i, :, lanes]) + t_mm(right, hb[1, j, :, lanes])
            grad = grad.reshape(4, 4, 16, 256)
            own[half, m] = grad
            rsend[half, m] = grad.astype(BF)
        sum_a[m] = [
            send(rsend.at[0, m, lax.rem(y + d, NY)], r1.at[0, m, n],
                 r1s.at[0, m, n], r1r.at[0, m, n], dev(dy=d))
            for n, d in enumerate((2, 1, 3))
        ]
        sum_b[m] = [
            send(rsend.at[1, m, :, lax.rem(z + d + NZ, 4)], r1.at[1, m, n],
                 r1s.at[1, m, n], r1r.at[1, m, n], dev(dz=d))
            for n, d in enumerate(near)
        ]

    back_queries(1, W_LATE)
    back_rest(1, W_LATE, B_LATE)
    exchange(1)

    for m in range(3):
        for copy in sum_a[m]:
            copy.wait_recv()
        total = own[0, m, y]
        for i in range(3):
            total = total + r1[0, m, i].astype(F32)
        acc[0, m] = total
        sd[0, m] = total.astype(BF)
        for copy in sum_b[m]:
            copy.wait_recv()
        total = own[1, m, :, zl]
        for i in range(3):
            total = total + r1[1, m, i].astype(F32)
        acc[1, m] = total
        sd[1, m] = total.astype(BF)
    two_a = [
        send(sd.at[0, :, lax.rem(z + d + NZ, 4)], r2.at[0, n], r2s.at[0, n], r2r.at[0, n], dev(dz=d))
        for n, d in enumerate(near)
    ]
    two_b = [
        send(sd.at[1, :, lax.rem(y + d, NY)], r2.at[1, n], r2s.at[1, n], r2r.at[1, n], dev(dy=d))
        for n, d in enumerate((2, 1, 3))
    ]

    x_relay(0)
    loads[8].wait()
    project(0)

    flip = 4 - 8 * lax.rem(zh, 2)
    third = {}

    def far_sum(half, step):
        fsend[half, step] = part[half].astype(BF)
        way = flip if half == step else -flip
        third[half] = send(
            fsend.at[half, step], rf.at[half, step], rfs.at[half, step], rfr.at[half, step], dev(dz=way)
        )

    for half, copies, place in ((0, two_a, zl), (1, two_b, y)):
        for copy in copies:
            copy.wait_recv()
        total = acc[half, :, place]
        for i in range(3):
            total = total + r2[half, i].astype(F32)
        part[half] = total
        for k in range(4):
            mine = jnp.where(zh == k, 1.0, 0.0)
            for m in range(3):
                rows = pl.ds(4 * k, 4)
                part[half, m, rows, :] = (
                    part[half, m, rows, :] + mine * adjv[m, :, pl.ds(half * 256, 256)]
                )
        far_sum(half, 0)

    gather_last(W_EARLY)
    for half in range(2):
        third[half].wait_recv()
        part[half] = part[half] + rf[half, 0].astype(F32)
        far_sum(half, 1)
    heads_send(1)
    for half in range(2):
        third[half].wait_recv()
        gath[B_EARLY, half, :, y, zl] = (part[half] + rf[half, 1].astype(F32)).astype(BF)
    gather_first(B_EARLY)
    gather_end(W_EARLY)
    gather_last(B_EARLY)
    forward(0, W_EARLY)
    back_queries(0, W_EARLY)
    heads_end(1)
    gather_end(B_EARLY)

    second(0, B_EARLY)
    back_rest(0, W_EARLY, B_EARLY)
    exchange(0)
    heads_send(0)
    heads_end(0)

    for copy in started:
        copy.wait_send()


def local(inputs, probe, address, payload, checkpoints, out_grad, adjoint, inner_rate):
    hbm = pl.BlockSpec(memory_space=pl.ANY)
    dma = pltpu.SemaphoreType.DMA
    scratch = [
        pltpu.VMEM((2, T, D), BF),
        pltpu.VMEM((3, D, DH), BF),
        pltpu.VMEM((D, 3 * DH), BF),
        pltpu.VMEM((4, DH, 3 * DH), BF),
        pltpu.VMEM((4, 2, 3, 4, 4, 16, 256), BF),
        pltpu.VMEM((3, 4, 3, 4, F), BF),
        pltpu.VMEM((3, 4, F), F32),
        pltpu.VMEM((3, 16, F), F32),
        pltpu.VMEM((2, T, DH), BF),
        pltpu.VMEM((2, 3, T, DH), BF),
        pltpu.VMEM((2, T, DH), BF),
        pltpu.VMEM((2, 9, T, F), F32),
        pltpu.VMEM((2, 9, T, F), BF),
        pltpu.VMEM((2, 3, 4, 4, 16, 256), F32),
        pltpu.VMEM((2, 3, 4, 4, 16, 256), BF),
        pltpu.VMEM((2, 3, 3, 4, 16, 256), BF),
        pltpu.VMEM((2, 3, 4, 16, 256), F32),
        pltpu.VMEM((2, 3, 4, 16, 256), BF),
        pltpu.VMEM((2, 3, 3, 16, 256), BF),
        pltpu.VMEM((2, 3, 16, 256), F32),
        pltpu.VMEM((2, 2, 3, 16, 256), BF),
        pltpu.VMEM((2, 2, 3, 16, 256), BF),
        pltpu.VMEM((2, T, 3 * DH), BF),
        pltpu.VMEM((2, T, 3 * DH), BF),
        pltpu.VMEM((2, 3, T, DH), BF),
        pltpu.VMEM((2, 3, T, DH), BF),
        dma((9,)),
    ]
    for shape in ((2, 7), (2, 4), (4, 2, 3), (4, 2, 3), (2, 3, 3), (2, 3), (2, 2), (6,), (2, 3)):
        scratch += [dma(shape), dma(shape)]
    return pl.pallas_call(
        kernel,
        name="meta_gradient",
        out_shape=jax.ShapeDtypeStruct((2, T, DH), BF),
        in_specs=[hbm] * 7 + [pl.BlockSpec(memory_space=pltpu.SMEM)],
        out_specs=pl.BlockSpec(memory_space=pltpu.VMEM),
        scratch_shapes=scratch,
        compiler_params=pltpu.CompilerParams(
            collective_id=0, has_side_effects=True, vmem_limit_bytes=60 * 2**20
        ),
    )(
        inputs,
        probe,
        address,
        payload,
        checkpoints.reshape(2, 3, 4, F),
        out_grad,
        adjoint.reshape(3, 4, F),
        inner_rate,
    )


def solution(mesh):
    split = Mesh(mesh.devices.reshape(NZ, NY, NX, NC), AXES)
    tok, head = ("z", "y"), ("x", "c")
    placed = (
        P(None, tok, head),
        P(None, head),
        P(None, head),
        P(None, head),
        P(None, None, head, tok, None),
        P(None, tok, head),
        P(None, head, tok, None),
        P(head),
    )
    return jax.shard_map(
        local, mesh=split, in_specs=placed, out_specs=P(None, tok, head), check_vma=False
    )
```

```python
import jax
import jax.numpy as jnp
from jax import lax
from jax.experimental import pallas as pl
from jax.experimental.pallas import tpu as pltpu
from jax.sharding import Mesh
from jax.sharding import PartitionSpec as P

AXES = ("z", "y", "x", "c")
NZ, NY, NX, NC = 16, 4, 4, 2
MESH = pl.DeviceIdType.MESH
BF = jnp.bfloat16
F32 = jnp.float32
T = 256
DH = 256
F = 512
D = 2048
W_LATE, B_LATE, W_EARLY, B_EARLY = 0, 1, 2, 3


def mm(a, b):
    return jnp.dot(a, b, preferred_element_type=F32)


def mm_t(a, b):
    return lax.dot_general(a, b, (((1,), (1,)), ((), ())), preferred_element_type=F32)


def t_mm(a, b):
    return lax.dot_general(a, b, (((0,), (0,)), ((), ())), preferred_element_type=F32)


def permutation():
    row = lax.broadcasted_iota(jnp.int32, (DH, DH), 0)
    place = lax.broadcasted_iota(jnp.int32, (DH, DH), 1)
    held = 64 * ((place // 4) % 4) + 16 * ((place // 16) % 4) + 4 * (place // 64) + place % 4
    return jnp.where(row == held, 1.0, 0.0).astype(BF)


def kernel(
    xin, pq, pk, pv, ck, og, adj, rate, out,
    xg, pr, pc, pp, gath, fb, adjv, tile, ogv, qkv, o_s, fw, hb, own, rsend,
    r1, acc, sd, r2, part, fsend, rf, gcat, gp, back, base, pb, ro,
    ls, xs, xr, fs, fr, as_, ar, bs, br, r1s, r1r, r2s, r2r, rfs, rfr, cs, cr, ps, pr_, hs, hr,
):
    z, y = lax.axis_index("z"), lax.axis_index("y")
    x, c = lax.axis_index("x"), lax.axis_index("c")

    def dev(dz=0, dy=0, dx=0, dc=0):
        return (
            lax.rem(z + dz + NZ, NZ), lax.rem(y + dy, NY), lax.rem(x + dx, NX), lax.rem(c + dc, NC)
        )

    zh, zl = z // 4, lax.rem(z, 4)
    skip = 4 * c - 2
    near = [1, -1, skip]

    barrier = pltpu.get_barrier_semaphore()
    partners = [dev(dz=d) for d in (4, -4, 2, -2, 1, -1)]
    partners += [dev(dy=d) for d in (1, 2, 3)] + [dev(dx=d) for d in (1, 2, 3)] + [dev(dc=1)]
    for partner in partners:
        pl.semaphore_signal(barrier, inc=1, device_id=partner, device_id_type=MESH)

    started = []

    def send(src, dst, ssem, rsem, device):
        copy = pltpu.make_async_remote_copy(
            src_ref=src, dst_ref=dst, send_sem=ssem, recv_sem=rsem,
            device_id=device, device_id_type=MESH,
        )
        copy.start()
        started.append(copy)
        return copy

    column = pl.multiple_of((x * 2 + c) * DH, DH)
    loads = [
        pltpu.make_async_copy(src, dst, ls.at[i])
        for i, (src, dst) in enumerate((
            (ck.at[1], fb.at[W_LATE, zh]),
            (adj, adjv),
            (ck.at[0], fb.at[W_EARLY, zh]),
            (xin.at[1], xg.at[1, :, pl.ds(column, DH)]),
            (pq, pr.at[0]),
            (pk, pr.at[1]),
            (pv, pr.at[2]),
            (og, ogv),
            (xin.at[0], xg.at[0, :, pl.ds(column, DH)]),
        ))
    ]
    for load in loads:
        load.start()
    for load in loads[:4]:
        load.wait()
    fb[B_LATE, zh] = adjv[...].astype(BF)

    pl.semaphore_wait(barrier, len(partners))

    far_copies = {}

    def far_send(i):
        piece = fb.at[i, zh]
        far_copies[i] = [
            send(piece, piece, fs.at[i, n], fr.at[i, n], dev(dz=d)) for n, d in enumerate((4, -4))
        ]

    def far_relay(i):
        for copy in far_copies[i]:
            copy.wait_recv()
        below = fb.at[i, lax.rem(zh + 3, 4), pl.ds(0, 1)]
        above = fb.at[i, lax.rem(zh + 1, 4), pl.ds(1, 2)]
        far_copies[i] = [
            send(below, below, fs.at[i, 2], fr.at[i, 2], dev(dz=4)),
            send(above, above, fs.at[i, 3], fr.at[i, 3], dev(dz=-4)),
        ]

    x_copies = {}

    def x_send(s):
        block = xg.at[s, :, pl.ds(column, DH)]
        x_copies[s] = [
            send(xin.at[s], block, xs.at[s, i], xr.at[s, i], dev(dx=d)) for i, d in enumerate((2, 1, 3))
        ]
        x_copies[s].append(send(xin.at[s], block, xs.at[s, 3], xr.at[s, 3], dev(dc=1)))

    far_send(W_LATE)
    far_send(B_LATE)
    x_send(1)
    far_send(W_EARLY)
    x_send(0)

    order = permutation()
    for i in range(3):
        loads[4 + i].wait()
        for j in range(8):
            rows = pl.ds(j * DH, DH)
            pc[rows, pl.ds(i * DH, DH)] = mm(pr[i, rows, :], order).astype(BF)

    far_relay(W_LATE)
    far_relay(B_LATE)
    far_relay(W_EARLY)

    other = 1 - c
    pc_copies = []
    for i in range(4):
        rows = pl.multiple_of((i * 2 + other) * DH, DH)
        pc_copies.append(
            send(pc.at[pl.ds(rows, DH), :], pp.at[i], cs.at[i], cr.at[i], dev(dc=1))
        )
    loads[7].wait()
    for s in range(2):
        o_s[s] = mm(ogv[s], order).astype(BF)

    first, last = {}, {}

    def to_near(block, ssem, rsem):
        return [send(block, block, ssem.at[i], rsem.at[i], dev(dz=d)) for i, d in enumerate(near)]

    def to_y(block, ssem, rsem):
        return [send(block, block, ssem.at[i], rsem.at[i], dev(dy=d)) for i, d in enumerate((2, 1, 3))]

    def gather_first(s, m=None):
        index = s if m is None else s + m
        mats = pl.ds(0, 3) if m is None else m
        first[index] = []
        for half, stage in ((0, to_near), (1, to_y)):
            block = gath.at[s, half, mats, y, zl]
            first[index] += stage(block, as_.at[index, half], ar.at[index, half])

    def gather_last(s, m=None):
        index = s if m is None else s + m
        mats = pl.ds(0, 3) if m is None else m
        for copy in first[index]:
            copy.wait_recv()
        last[index] = to_y(gath.at[s, 0, mats, y], bs.at[index, 0], br.at[index, 0])
        last[index] += to_near(gath.at[s, 1, mats, :, zl], bs.at[index, 1], br.at[index, 1])

    def gather_end(s):
        for copy in last[s]:
            copy.wait_recv()

    def far_end(i):
        for copy in far_copies[i]:
            copy.wait_recv()

    def assemble(s):
        for m in range(3):
            for k in range(4):
                tile[m, pl.ds(4 * k, 4), :] = fb[s, k, m].astype(F32)
            gath[s, 0, m, y, zl] = tile[m, :, pl.ds(0, 256)].astype(BF)
            gath[s, 1, m, y, zl] = tile[m, :, pl.ds(256, 256)].astype(BF)

    relays = {}

    def x_relay(s):
        relays[s] = []
        for i, d in enumerate((2, 1, 3)):
            x_copies[s][i].wait_recv()
            source = pl.multiple_of((lax.rem(x + 4 - d, NX) * 2 + c) * DH, DH)
            block = xg.at[s, :, pl.ds(source, DH)]
            relays[s].append(send(block, block, xs.at[s, 4 + i], xr.at[s, 4 + i], dev(dc=1)))

    def project(s):
        for copy in [x_copies[s][3]] + relays[s]:
            copy.wait_recv()
        for i in range(3):
            qkv[s, i] = mm(xg[s], pc[:, pl.ds(i * DH, DH)]).astype(BF)

    factor = rate[0] / 16384.0

    def weight(s, half, m):
        return gath[s, half, m].reshape(DH, 256)

    def ahead(rows, s, m, to):
        for half in range(2):
            fw[to[0], to[1], :, pl.ds(half * 256, 256)] = mm(rows, weight(s, half, m))

    def behind(s, i, w, m):
        return mm_t(hb[s, i, :, pl.ds(0, 256)], weight(w, 0, m)) + mm_t(
            hb[s, i, :, pl.ds(256, 256)], weight(w, 1, m)
        )

    def forward(s, w):
        q, k, v = qkv[s, 0], qkv[s, 1], qkv[s, 2]
        ahead(q, w, 0, (s, 0))
        ahead(q, w, 1, (s, 1))
        ahead(o_s[s], w, 2, (s, 2))
        ahead(k, w, 0, (s, 3))
        ahead(k, w, 1, (s, 4))
        ahead(v, w, 2, (s, 5))

        @pl.loop(0, T // 16)
        def _(step):
            rows = pl.ds(pl.multiple_of(step * 16, 16), 16)
            gate, lift, back = fw[s, 0, rows, :], fw[s, 1, rows, :], fw[s, 2, rows, :]
            g = jax.nn.sigmoid(gate)
            act = gate * g
            if s > 0:
                hb[s, 0, rows, :] = (act * lift).astype(BF)
            hb[s, 1, rows, :] = (back * lift * (g * (1.0 + gate * (1.0 - g)))).astype(BF)
            hb[s, 2, rows, :] = (back * act).astype(BF)
            gate, u, e = fw[s, 3, rows, :], fw[s, 4, rows, :], fw[s, 5, rows, :]
            g = jax.nn.sigmoid(gate)
            act = factor * gate * g
            slope = factor * (g * (1.0 + gate * (1.0 - g)))
            bend = factor * (g * (1.0 - g) * (2.0 + gate * (1.0 - 2.0 * g)))
            us = u * slope
            fw[s, 0, rows, :] = us
            fw[s, 1, rows, :] = e * u * bend
            fw[s, 2, rows, :] = e * slope
            fw[s, 3, rows, :] = act
            hb[s, 6, rows, :] = (act * u).astype(BF)
            hb[s, 7, rows, :] = (e * us).astype(BF)
            hb[s, 8, rows, :] = (e * act).astype(BF)

    def sides(s, b, m):
        ahead(qkv[s, 1] if m < 2 else qkv[s, 2], b, m, (s, (7, 8, 6)[m]))

    def second(s):
        @pl.loop(0, T // 16)
        def _(step):
            rows = pl.ds(pl.multiple_of(step * 16, 16), 16)
            pull, one, three = fw[s, 6, rows, :], fw[s, 7, rows, :], fw[s, 8, rows, :]
            us, eub, es, act = (fw[s, i, rows, :] for i in range(4))
            hb[s, 3, rows, :] = (us * pull + one * eub + three * es).astype(BF)
            hb[s, 4, rows, :] = (act * pull + one * es).astype(BF)
            hb[s, 5, rows, :] = (one * us + three * act).astype(BF)

    def back_queries(s, w):
        grad = behind(s, 1, w, 0) + behind(s, 2, w, 1)
        gcat[s, :, pl.ds(0, DH)] = grad.astype(BF)

    def back_sides(s, b):
        back[0] = behind(s, 7, b, 0) + behind(s, 8, b, 1)
        back[1] = behind(s, 6, b, 2)

    def back_rest(s, w):
        grad = behind(s, 3, w, 0) + behind(s, 4, w, 1) + back[0]
        gcat[s, :, pl.ds(DH, DH)] = grad.astype(BF)
        grad = behind(s, 5, w, 2) + back[1]
        gcat[s, :, pl.ds(2 * DH, DH)] = grad.astype(BF)

    pair = {}
    query_part, rest_part = pl.ds(0, DH), pl.ds(DH, 2 * DH)

    def exchange(s, i, lanes):
        pair[s, i] = send(
            gcat.at[s, :, lanes], gp.at[s, :, lanes], ps.at[s, i], pr_.at[s, i], dev(dc=1)
        )

    heads = {}
    steps = (2, 1, 3, 0)

    def own_term(s, step, lanes):
        rows = pl.multiple_of((lax.rem(x + step, NX) * 2 + c) * DH, DH)
        return mm_t(gcat[s, :, lanes], pc[pl.ds(rows, DH), lanes])

    def pair_term(s, step, lanes):
        return mm_t(gp[s, :, lanes], pp[lax.rem(x + step, NX), :, lanes])

    def heads_queries(s):
        pair[s, 0].wait_recv()
        for i, step in enumerate(steps):
            base[i] = own_term(s, step, query_part) + pair_term(s, step, query_part)

    def heads_send(s):
        for i, step in enumerate(steps):
            base[i] = base[i] + own_term(s, step, rest_part)
        pair[s, 1].wait_recv()
        heads[s] = []
        for i, step in enumerate(steps[:3]):
            pb[s, i] = (base[i] + pair_term(s, step, rest_part)).astype(BF)
            heads[s].append(
                send(pb.at[s, i], ro.at[s, i], hs.at[s, i], hr.at[s, i], dev(dx=step))
            )
        base[3] = base[3] + pair_term(s, 0, rest_part)

    def heads_end(s):
        total = base[3]
        for i in range(3):
            heads[s][i].wait_recv()
            total = total + ro[s, i].astype(F32)
        out[s] = total.astype(BF)

    x_relay(1)
    for s in (W_LATE, B_LATE, W_EARLY):
        far_end(s)
        assemble(s)
        gather_first(s)
    project(1)
    gather_last(W_LATE)
    gather_last(B_LATE)
    x_relay(0)
    loads[8].wait()
    project(0)
    gather_end(W_LATE)
    gather_last(W_EARLY)
    forward(1, W_LATE)
    back_queries(1, W_LATE)
    gather_end(B_LATE)
    for m in range(3):
        sides(1, B_LATE, m)
    second(1)

    terms = (
        (qkv[1, 1], 3, qkv[1, 0], 1),
        (qkv[1, 1], 4, qkv[1, 0], 2),
        (qkv[1, 2], 5, o_s[1], 0),
    )
    sum_a, sum_b = {}, {}
    for m, (left, i, right, j) in enumerate(terms):
        for half in range(2):
            lanes = pl.ds(half * 256, 256)
            grad = t_mm(left, hb[1, i, :, lanes]) + t_mm(right, hb[1, j, :, lanes])
            grad = grad.reshape(4, 4, 16, 256)
            own[half, m] = grad
            rsend[half, m] = grad.astype(BF)
        sum_a[m] = [
            send(rsend.at[0, m, lax.rem(y + d, NY)], r1.at[0, m, n],
                 r1s.at[0, m, n], r1r.at[0, m, n], dev(dy=d))
            for n, d in enumerate((2, 1, 3))
        ]
        sum_b[m] = [
            send(rsend.at[1, m, :, lax.rem(z + d + NZ, 4)], r1.at[1, m, n],
                 r1s.at[1, m, n], r1r.at[1, m, n], dev(dz=d))
            for n, d in enumerate(near)
        ]

    exchange(1, 0, query_part)
    back_sides(1, B_LATE)
    back_rest(1, W_LATE)
    exchange(1, 1, rest_part)

    two = {}
    for m in range(3):
        for copy in sum_a[m]:
            copy.wait_recv()
        total = own[0, m, y]
        for i in range(3):
            total = total + r1[0, m, i].astype(F32)
        acc[0, m] = total
        sd[0, m] = total.astype(BF)
        two[0, m] = [
            send(sd.at[0, m, lax.rem(z + d + NZ, 4)], r2.at[0, m, n],
                 r2s.at[0, m, n], r2r.at[0, m, n], dev(dz=d))
            for n, d in enumerate(near)
        ]
        for copy in sum_b[m]:
            copy.wait_recv()
        total = own[1, m, :, zl]
        for i in range(3):
            total = total + r1[1, m, i].astype(F32)
        acc[1, m] = total
        sd[1, m] = total.astype(BF)
        two[1, m] = [
            send(sd.at[1, m, lax.rem(y + d, NY)], r2.at[1, m, n],
                 r2s.at[1, m, n], r2r.at[1, m, n], dev(dy=d))
            for n, d in enumerate((2, 1, 3))
        ]

    flip = 4 - 8 * lax.rem(zh, 2)
    third = {}

    def far_sum(half, m, step):
        fsend[half, step, m] = part[half, m].astype(BF)
        way = flip if half == step else -flip
        third[half, m] = send(
            fsend.at[half, step, m], rf.at[half, step, m],
            rfs.at[half, step, m], rfr.at[half, step, m], dev(dz=way)
        )

    for m in range(3):
        for half, place in ((0, zl), (1, y)):
            for copy in two[half, m]:
                copy.wait_recv()
            total = acc[half, m, place]
            for i in range(3):
                total = total + r2[half, m, i].astype(F32)
            part[half, m] = total
            for k in range(4):
                mine = jnp.where(zh == k, 1.0, 0.0)
                rows = pl.ds(4 * k, 4)
                part[half, m, rows, :] = (
                    part[half, m, rows, :] + mine * adjv[m, :, pl.ds(half * 256, 256)]
                )
            far_sum(half, m, 0)

    gather_end(W_EARLY)
    forward(0, W_EARLY)

    for m in range(3):
        for half in range(2):
            third[half, m].wait_recv()
            part[half, m] = part[half, m] + rf[half, 0, m].astype(F32)
            far_sum(half, m, 1)

    for copy in pc_copies:
        copy.wait_recv()
    back_queries(0, W_EARLY)
    exchange(0, 0, query_part)
    heads_queries(1)
    heads_send(1)

    for m in range(3):
        for half in range(2):
            third[half, m].wait_recv()
            total = part[half, m] + rf[half, 1, m].astype(F32)
            gath[B_EARLY, half, m, y, zl] = total.astype(BF)
        gather_first(B_EARLY, m)
    heads_end(1)
    for m in range(3):
        gather_last(B_EARLY, m)
    heads_queries(0)
    for m in range(3):
        gather_end(B_EARLY + m)
        sides(0, B_EARLY, m)

    second(0)
    back_sides(0, B_EARLY)
    back_rest(0, W_EARLY)
    exchange(0, 1, rest_part)
    heads_send(0)
    heads_end(0)

    for copy in started:
        copy.wait_send()


def local(inputs, probe, address, payload, checkpoints, out_grad, adjoint, inner_rate):
    hbm = pl.BlockSpec(memory_space=pl.ANY)
    dma = pltpu.SemaphoreType.DMA
    scratch = [
        pltpu.VMEM((2, T, D), BF),
        pltpu.VMEM((3, D, DH), BF),
        pltpu.VMEM((D, 3 * DH), BF),
        pltpu.VMEM((4, DH, 3 * DH), BF),
        pltpu.VMEM((4, 2, 3, 4, 4, 16, 256), BF),
        pltpu.VMEM((3, 4, 3, 4, F), BF),
        pltpu.VMEM((3, 4, F), F32),
        pltpu.VMEM((3, 16, F), F32),
        pltpu.VMEM((2, T, DH), BF),
        pltpu.VMEM((2, 3, T, DH), BF),
        pltpu.VMEM((2, T, DH), BF),
        pltpu.VMEM((2, 9, T, F), F32),
        pltpu.VMEM((2, 9, T, F), BF),
        pltpu.VMEM((2, 3, 4, 4, 16, 256), F32),
        pltpu.VMEM((2, 3, 4, 4, 16, 256), BF),
        pltpu.VMEM((2, 3, 3, 4, 16, 256), BF),
        pltpu.VMEM((2, 3, 4, 16, 256), F32),
        pltpu.VMEM((2, 3, 4, 16, 256), BF),
        pltpu.VMEM((2, 3, 3, 16, 256), BF),
        pltpu.VMEM((2, 3, 16, 256), F32),
        pltpu.VMEM((2, 2, 3, 16, 256), BF),
        pltpu.VMEM((2, 2, 3, 16, 256), BF),
        pltpu.VMEM((2, T, 3 * DH), BF),
        pltpu.VMEM((2, T, 3 * DH), BF),
        pltpu.VMEM((2, T, DH), F32),
        pltpu.VMEM((4, T, DH), F32),
        pltpu.VMEM((2, 3, T, DH), BF),
        pltpu.VMEM((2, 3, T, DH), BF),
        dma((9,)),
    ]
    for shape in ((2, 7), (3, 4), (6, 2, 3), (6, 2, 3), (2, 3, 3), (2, 3, 3), (2, 2, 3), (4,), (2, 2), (2, 3)):
        scratch += [dma(shape), dma(shape)]
    return pl.pallas_call(
        kernel,
        name="meta_gradient",
        out_shape=jax.ShapeDtypeStruct((2, T, DH), BF),
        in_specs=[hbm] * 7 + [pl.BlockSpec(memory_space=pltpu.SMEM)],
        out_specs=pl.BlockSpec(memory_space=pltpu.VMEM),
        scratch_shapes=scratch,
        compiler_params=pltpu.CompilerParams(
            collective_id=0, has_side_effects=True, vmem_limit_bytes=60 * 2**20
        ),
    )(
        inputs,
        probe,
        address,
        payload,
        checkpoints.reshape(2, 3, 4, F),
        out_grad,
        adjoint.reshape(3, 4, F),
        inner_rate,
    )


def solution(mesh):
    split = Mesh(mesh.devices.reshape(NZ, NY, NX, NC), AXES)
    tok, head = ("z", "y"), ("x", "c")
    placed = (
        P(None, tok, head),
        P(None, head),
        P(None, head),
        P(None, head),
        P(None, None, head, tok, None),
        P(None, tok, head),
        P(None, head, tok, None),
        P(head),
    )
    return jax.shard_map(
        local, mesh=split, in_specs=placed, out_specs=P(None, tok, head), check_vma=False
    )
```

```python
import jax
import jax.numpy as jnp
from jax import lax
from jax.experimental import pallas as pl
from jax.experimental.pallas import tpu as pltpu
from jax.sharding import Mesh
from jax.sharding import PartitionSpec as P

AXES = ("z", "y", "x", "c")
NZ, NY, NX, NC = 16, 4, 4, 2
MESH = pl.DeviceIdType.MESH
BF = jnp.bfloat16
F32 = jnp.float32
T = 256
DH = 256
F = 512
D = 2048
W_LATE, B_LATE, W_EARLY, B_EARLY = 0, 1, 2, 3


def mm(a, b):
    return jnp.dot(a, b, preferred_element_type=F32)


def mm_t(a, b):
    return lax.dot_general(a, b, (((1,), (1,)), ((), ())), preferred_element_type=F32)


def permutation():
    row = lax.broadcasted_iota(jnp.int32, (DH, DH), 0)
    place = lax.broadcasted_iota(jnp.int32, (DH, DH), 1)
    held = 64 * ((place // 4) % 4) + 16 * ((place // 16) % 4) + 4 * (place // 64) + place % 4
    return jnp.where(row == held, 1.0, 0.0).astype(BF)


def kernel(
    xin, pq, pk, pv, ck, og, adj, rate, out,
    xg, pr, pc, pp, gath, fb, adjv, tile, ogv, qkv, o_s, fw, hb, own, rsend,
    turned, r1, acc, sd, r2, part, fsend, rf, gcat, gp, back, base, pb, ro,
    ls, xs, xr, fs, fr, as_, ar, bs, br, r1s, r1r, r2s, r2r, rfs, rfr, cs, cr, ps, pr_, hs, hr,
):
    z, y = lax.axis_index("z"), lax.axis_index("y")
    x, c = lax.axis_index("x"), lax.axis_index("c")

    def dev(dz=0, dy=0, dx=0, dc=0):
        return (
            lax.rem(z + dz + NZ, NZ), lax.rem(y + dy, NY), lax.rem(x + dx, NX), lax.rem(c + dc, NC)
        )

    zh, zl = z // 4, lax.rem(z, 4)
    odd, pair_row = lax.rem(zh, 2), zh // 2
    flip = 4 - 8 * odd
    skip = 4 * c - 2
    near = [1, -1, skip]

    barrier = pltpu.get_barrier_semaphore()
    partners = [dev(dz=d) for d in (4, -4, 2, -2, 1, -1)]
    partners += [dev(dy=d) for d in (1, 2, 3)] + [dev(dx=d) for d in (1, 2, 3)] + [dev(dc=1)]
    for partner in partners:
        pl.semaphore_signal(barrier, inc=1, device_id=partner, device_id_type=MESH)

    started = []

    def send(src, dst, ssem, rsem, device):
        copy = pltpu.make_async_remote_copy(
            src_ref=src, dst_ref=dst, send_sem=ssem, recv_sem=rsem,
            device_id=device, device_id_type=MESH,
        )
        copy.start()
        started.append(copy)
        return copy

    column = pl.multiple_of((x * 2 + c) * DH, DH)
    loads = [
        pltpu.make_async_copy(src, dst, ls.at[i])
        for i, (src, dst) in enumerate((
            (ck.at[1], fb.at[W_LATE, odd]),
            (adj, adjv),
            (ck.at[0], fb.at[W_EARLY, odd]),
            (xin.at[1], xg.at[1, :, pl.ds(column, DH)]),
            (pq, pr.at[0]),
            (pk, pr.at[1]),
            (pv, pr.at[2]),
            (og, ogv),
            (xin.at[0], xg.at[0, :, pl.ds(column, DH)]),
        ))
    ]
    for load in loads:
        load.start()
    pl.semaphore_wait(barrier, len(partners))

    far_one, far_two = {}, {}

    def far_send(s, piece):
        far_one[s] = send(piece, fb.at[s, odd], fs.at[s, 0], fr.at[s, 0], dev(dz=flip))

    x_copies = {}

    def x_send(s):
        block = xg.at[s, :, pl.ds(column, DH)]
        x_copies[s] = [
            send(xin.at[s], block, xs.at[s, i], xr.at[s, i], dev(dx=d)) for i, d in enumerate((2, 1, 3))
        ]
        x_copies[s].append(send(xin.at[s], block, xs.at[s, 3], xr.at[s, 3], dev(dc=1)))

    far_send(W_LATE, ck.at[1])
    loads[1].wait()
    fb[B_LATE, odd] = adjv[...].astype(BF)
    far_send(B_LATE, fb.at[B_LATE, odd])
    x_send(1)
    for i in (0, 2, 3):
        loads[i].wait()

    order = permutation()
    for i in range(3):
        loads[4 + i].wait()
        for j in range(8):
            rows = pl.ds(j * DH, DH)
            pc[rows, pl.ds(i * DH, DH)] = mm(pr[i, rows, :], order).astype(BF)

    def rows8(of):
        return pl.ds(pl.multiple_of(8 * of, 8), 8)

    def assemble(s):
        far_one[s].wait_recv()
        for m in range(3):
            for k in range(2):
                tile[m, pl.ds(4 * k, 4), :] = fb[s, k, m].astype(F32)
        for half in range(2):
            rows = tile[:, :, pl.ds(half * 256, 256)].astype(BF)
            for k in range(2):

                @pl.when(pair_row == k)
                def _():
                    gath[s, half, :, y, zl, pl.ds(8 * k, 8), :] = rows

        block = gath.at[s, :, :, y, zl, rows8(pair_row), :]
        far_two[s] = send(block, block, fs.at[s, 1], fr.at[s, 1], dev(dz=-flip))

    other = 1 - c
    first, last = {}, {}

    def to_near(block, ssem, rsem):
        return [send(block, block, ssem.at[i], rsem.at[i], dev(dz=d)) for i, d in enumerate(near)]

    def to_y(block, ssem, rsem):
        return [send(block, block, ssem.at[i], rsem.at[i], dev(dy=d)) for i, d in enumerate((2, 1, 3))]

    members = [z] + [lax.rem(z + d + NZ, NZ) for d in (1, -1, -skip)]

    def part_first(s, late):
        if late:
            far_two[s].wait_recv()
        index = 2 * s + late
        rows = rows8(1 - pair_row if late else pair_row)
        first[index] = to_near(gath.at[s, 0, :, y, zl, rows, :], as_.at[index, 0], ar.at[index, 0])
        first[index] += to_y(gath.at[s, 1, :, y, zl, rows, :], as_.at[index, 1], ar.at[index, 1])

    def part_last(s, late):
        index = 2 * s + late
        for copy in first[index]:
            copy.wait_recv()
        last[index] = []
        for n, member in enumerate(members):
            of = member // 8
            block = gath.at[s, 0, :, y, lax.rem(member, 4), rows8(1 - of if late else of), :]
            last[index] += to_y(block, bs.at[index, n], br.at[index, n])
        block = gath.at[s, 1, :, :, zl, rows8(1 - pair_row if late else pair_row), :]
        last[index] += to_near(block, bs.at[index, 4], br.at[index, 4])

    def whole_first(s):
        first[6] = to_near(gath.at[s, 0, :, y, zl], as_.at[6, 0], ar.at[6, 0])
        first[6] += to_y(gath.at[s, 1, :, y, zl], as_.at[6, 1], ar.at[6, 1])

    def whole_last(s):
        for copy in first[6]:
            copy.wait_recv()
        last[6] = to_y(gath.at[s, 0, :, y], bs.at[6, 0], br.at[6, 0])
        last[6] += to_near(gath.at[s, 1, :, :, zl], bs.at[6, 4], br.at[6, 4])

    def gather_end(s):
        for index in (6,) if s == B_EARLY else (2 * s, 2 * s + 1):
            for copy in last[index]:
                copy.wait_recv()

    relays = {}

    def x_relay(s):
        relays[s] = []
        for i, d in enumerate((2, 1, 3)):
            x_copies[s][i].wait_recv()
            source = pl.multiple_of((lax.rem(x + 4 - d, NX) * 2 + c) * DH, DH)
            block = xg.at[s, :, pl.ds(source, DH)]
            relays[s].append(send(block, block, xs.at[s, 4 + i], xr.at[s, 4 + i], dev(dc=1)))

    def project(s):
        for copy in [x_copies[s][3]] + relays[s]:
            copy.wait_recv()
        for i in range(3):
            qkv[s, i] = mm(xg[s], pc[:, pl.ds(i * DH, DH)]).astype(BF)

    factor = rate[0] / 16384.0

    def weight(s, half, m):
        return gath[s, half, m].reshape(DH, 256)

    def ahead(rows, s, m, to):
        for half in range(2):
            fw[to[0], to[1], :, pl.ds(half * 256, 256)] = mm(rows, weight(s, half, m))

    def behind(s, i, w, m):
        return mm_t(hb[s, i, :, pl.ds(0, 256)], weight(w, 0, m)) + mm_t(
            hb[s, i, :, pl.ds(256, 256)], weight(w, 1, m)
        )

    def forward(s, w):
        q, k, v = qkv[s, 0], qkv[s, 1], qkv[s, 2]
        ahead(q, w, 0, (s, 0))
        ahead(q, w, 1, (s, 1))
        ahead(o_s[s], w, 2, (s, 2))
        ahead(k, w, 0, (s, 3))
        ahead(k, w, 1, (s, 4))
        ahead(v, w, 2, (s, 5))

        @pl.loop(0, T // 16)
        def _(step):
            rows = pl.ds(pl.multiple_of(step * 16, 16), 16)
            gate, lift, back = fw[s, 0, rows, :], fw[s, 1, rows, :], fw[s, 2, rows, :]
            g = jax.nn.sigmoid(gate)
            act = gate * g
            if s > 0:
                hb[s, 0, rows, :] = (act * lift).astype(BF)
            hb[s, 1, rows, :] = (back * lift * (g * (1.0 + gate * (1.0 - g)))).astype(BF)
            hb[s, 2, rows, :] = (back * act).astype(BF)
            gate, u, e = fw[s, 3, rows, :], fw[s, 4, rows, :], fw[s, 5, rows, :]
            g = jax.nn.sigmoid(gate)
            act = factor * gate * g
            slope = factor * (g * (1.0 + gate * (1.0 - g)))
            bend = factor * (g * (1.0 - g) * (2.0 + gate * (1.0 - 2.0 * g)))
            us = u * slope
            fw[s, 0, rows, :] = us
            fw[s, 1, rows, :] = e * u * bend
            fw[s, 2, rows, :] = e * slope
            fw[s, 3, rows, :] = act
            hb[s, 6, rows, :] = (act * u).astype(BF)
            hb[s, 7, rows, :] = (e * us).astype(BF)
            hb[s, 8, rows, :] = (e * act).astype(BF)

    def sides(s, b, m):
        ahead(qkv[s, 1] if m < 2 else qkv[s, 2], b, m, (s, (7, 8, 6)[m]))

    def second(s):
        @pl.loop(0, T // 16)
        def _(step):
            rows = pl.ds(pl.multiple_of(step * 16, 16), 16)
            pull, one, three = fw[s, 6, rows, :], fw[s, 7, rows, :], fw[s, 8, rows, :]
            us, eub, es, act = (fw[s, i, rows, :] for i in range(4))
            hb[s, 3, rows, :] = (us * pull + one * eub + three * es).astype(BF)
            hb[s, 4, rows, :] = (act * pull + one * es).astype(BF)
            hb[s, 5, rows, :] = (one * us + three * act).astype(BF)

    def back_queries(s, w):
        grad = behind(s, 1, w, 0) + behind(s, 2, w, 1)
        gcat[s, :, pl.ds(0, DH)] = grad.astype(BF)

    def back_sides(s, b):
        back[0] = behind(s, 7, b, 0) + behind(s, 8, b, 1)
        back[1] = behind(s, 6, b, 2)

    def back_rest(s, w):
        grad = behind(s, 3, w, 0) + behind(s, 4, w, 1) + back[0]
        gcat[s, :, pl.ds(DH, DH)] = grad.astype(BF)
        grad = behind(s, 5, w, 2) + back[1]
        gcat[s, :, pl.ds(2 * DH, DH)] = grad.astype(BF)

    pair = {}
    query_part, rest_part = pl.ds(0, DH), pl.ds(DH, 2 * DH)

    def exchange(s, i, lanes):
        pair[s, i] = send(
            gcat.at[s, :, lanes], gp.at[s, :, lanes], ps.at[s, i], pr_.at[s, i], dev(dc=1)
        )

    heads = {}
    steps = (2, 1, 3, 0)

    def own_term(s, step, lanes):
        rows = pl.multiple_of((lax.rem(x + step, NX) * 2 + c) * DH, DH)
        return mm_t(gcat[s, :, lanes], pc[pl.ds(rows, DH), lanes])

    def pair_term(s, step, lanes):
        return mm_t(gp[s, :, lanes], pp[lax.rem(x + step, NX), :, lanes])

    def heads_queries(s):
        pair[s, 0].wait_recv()
        for i, step in enumerate(steps):
            base[i] = own_term(s, step, query_part) + pair_term(s, step, query_part)

    def heads_send(s):
        for i, step in enumerate(steps):
            base[i] = base[i] + own_term(s, step, rest_part)
        pair[s, 1].wait_recv()
        heads[s] = []
        for i, step in enumerate(steps[:3]):
            pb[s, i] = (base[i] + pair_term(s, step, rest_part)).astype(BF)
            heads[s].append(
                send(pb.at[s, i], ro.at[s, i], hs.at[s, i], hr.at[s, i], dev(dx=step))
            )
        base[3] = base[3] + pair_term(s, 0, rest_part)

    def heads_end(s):
        total = base[3]
        for i in range(3):
            heads[s][i].wait_recv()
            total = total + ro[s, i].astype(F32)
        out[s] = total.astype(BF)

    assemble(W_LATE)
    part_first(W_LATE, 0)
    assemble(B_LATE)
    part_first(B_LATE, 0)
    far_send(W_EARLY, ck.at[0])
    x_send(0)
    pc_copies = []
    for i in range(4):
        rows = pl.multiple_of((i * 2 + other) * DH, DH)
        pc_copies.append(
            send(pc.at[pl.ds(rows, DH), :], pp.at[i], cs.at[i], cr.at[i], dev(dc=1))
        )
    loads[7].wait()
    for s in range(2):
        o_s[s] = mm(ogv[s], order).astype(BF)
    part_last(W_LATE, 0)
    part_first(W_LATE, 1)
    part_first(B_LATE, 1)
    part_last(B_LATE, 0)
    x_relay(1)
    assemble(W_EARLY)
    part_first(W_EARLY, 0)
    project(1)
    part_last(W_LATE, 1)
    part_last(B_LATE, 1)
    part_first(W_EARLY, 1)
    for i, rows in enumerate((qkv[1, 1], qkv[1, 0], qkv[1, 2], o_s[1])):
        turned[i] = rows.T
    x_relay(0)
    loads[8].wait()
    project(0)
    gather_end(W_LATE)
    part_last(W_EARLY, 0)
    forward(1, W_LATE)
    back_queries(1, W_LATE)
    part_last(W_EARLY, 1)
    gather_end(B_LATE)
    for m in range(3):
        sides(1, B_LATE, m)
    second(1)

    terms = ((0, 3, 1, 1), (0, 4, 1, 2), (2, 5, 3, 0))
    sum_a, sum_b = {}, {}
    for m, (left, i, right, j) in enumerate(terms):
        for half in range(2):
            lanes = pl.ds(half * 256, 256)
            grad = mm(turned[left], hb[1, i, :, lanes]) + mm(turned[right], hb[1, j, :, lanes])
            grad = grad.reshape(4, 4, 16, 256)
            own[half, m] = grad
            rsend[half, m] = grad.astype(BF)
        sum_a[m] = [
            send(rsend.at[0, m, lax.rem(y + d, NY)], r1.at[0, m, n],
                 r1s.at[0, m, n], r1r.at[0, m, n], dev(dy=d))
            for n, d in enumerate((2, 1, 3))
        ]
        sum_b[m] = [
            send(rsend.at[1, m, :, lax.rem(z + d + NZ, 4)], r1.at[1, m, n],
                 r1s.at[1, m, n], r1r.at[1, m, n], dev(dz=d))
            for n, d in enumerate(near)
        ]

    exchange(1, 0, query_part)
    back_sides(1, B_LATE)
    back_rest(1, W_LATE)
    exchange(1, 1, rest_part)

    for m in range(3):
        for copy in sum_a[m]:
            copy.wait_recv()
        total = own[0, m, y]
        for i in range(3):
            total = total + r1[0, m, i].astype(F32)
        acc[0, m] = total
        sd[0, m] = total.astype(BF)
    two_a = [
        send(sd.at[0, :, lax.rem(z + d + NZ, 4)], r2.at[0, n], r2s.at[0, n], r2r.at[0, n], dev(dz=d))
        for n, d in enumerate(near)
    ]
    for m in range(3):
        for copy in sum_b[m]:
            copy.wait_recv()
        total = own[1, m, :, zl]
        for i in range(3):
            total = total + r1[1, m, i].astype(F32)
        acc[1, m] = total
        sd[1, m] = total.astype(BF)
    two_b = [
        send(sd.at[1, :, lax.rem(y + d, NY)], r2.at[1, n], r2s.at[1, n], r2r.at[1, n], dev(dy=d))
        for n, d in enumerate((2, 1, 3))
    ]

    third = {}

    def far_sum(half, step):
        fsend[half, step] = part[half].astype(BF)
        way = flip if half == step else -flip
        third[half] = send(
            fsend.at[half, step], rf.at[half, step], rfs.at[half, step], rfr.at[half, step], dev(dz=way)
        )

    for half, copies, place in ((0, two_a, zl), (1, two_b, y)):
        for copy in copies:
            copy.wait_recv()
        total = acc[half, :, place]
        for i in range(3):
            total = total + r2[half, i].astype(F32)
        part[half] = total
        for k in range(4):
            mine = jnp.where(zh == k, 1.0, 0.0)
            for m in range(3):
                rows = pl.ds(4 * k, 4)
                part[half, m, rows, :] = (
                    part[half, m, rows, :] + mine * adjv[m, :, pl.ds(half * 256, 256)]
                )
        far_sum(half, 0)

    gather_end(W_EARLY)
    forward(0, W_EARLY)

    for half in range(2):
        third[half].wait_recv()
        part[half] = part[half] + rf[half, 0].astype(F32)
        far_sum(half, 1)

    for copy in pc_copies:
        copy.wait_recv()
    back_queries(0, W_EARLY)
    exchange(0, 0, query_part)
    heads_queries(1)
    heads_send(1)

    for half in range(2):
        third[half].wait_recv()
        gath[B_EARLY, half, :, y, zl] = (part[half] + rf[half, 1].astype(F32)).astype(BF)
    whole_first(B_EARLY)
    heads_end(1)
    whole_last(B_EARLY)
    heads_queries(0)
    gather_end(B_EARLY)
    for m in range(3):
        sides(0, B_EARLY, m)

    second(0)
    back_sides(0, B_EARLY)
    back_rest(0, W_EARLY)
    exchange(0, 1, rest_part)
    heads_send(0)
    heads_end(0)

    for copy in started:
        copy.wait_send()


def local(inputs, probe, address, payload, checkpoints, out_grad, adjoint, inner_rate):
    hbm = pl.BlockSpec(memory_space=pl.ANY)
    dma = pltpu.SemaphoreType.DMA
    scratch = [
        pltpu.VMEM((2, T, D), BF),
        pltpu.VMEM((3, D, DH), BF),
        pltpu.VMEM((D, 3 * DH), BF),
        pltpu.VMEM((4, DH, 3 * DH), BF),
        pltpu.VMEM((4, 2, 3, 4, 4, 16, 256), BF),
        pltpu.VMEM((3, 2, 3, 4, F), BF),
        pltpu.VMEM((3, 4, F), F32),
        pltpu.VMEM((3, 8, F), F32),
        pltpu.VMEM((2, T, DH), BF),
        pltpu.VMEM((2, 3, T, DH), BF),
        pltpu.VMEM((2, T, DH), BF),
        pltpu.VMEM((2, 9, T, F), F32),
        pltpu.VMEM((2, 9, T, F), BF),
        pltpu.VMEM((2, 3, 4, 4, 16, 256), F32),
        pltpu.VMEM((2, 3, 4, 4, 16, 256), BF),
        pltpu.VMEM((4, DH, T), BF),
        pltpu.VMEM((2, 3, 3, 4, 16, 256), BF),
        pltpu.VMEM((2, 3, 4, 16, 256), F32),
        pltpu.VMEM((2, 3, 4, 16, 256), BF),
        pltpu.VMEM((2, 3, 3, 16, 256), BF),
        pltpu.VMEM((2, 3, 16, 256), F32),
        pltpu.VMEM((2, 2, 3, 16, 256), BF),
        pltpu.VMEM((2, 2, 3, 16, 256), BF),
        pltpu.VMEM((2, T, 3 * DH), BF),
        pltpu.VMEM((2, T, 3 * DH), BF),
        pltpu.VMEM((2, T, DH), F32),
        pltpu.VMEM((4, T, DH), F32),
        pltpu.VMEM((2, 3, T, DH), BF),
        pltpu.VMEM((2, 3, T, DH), BF),
        dma((9,)),
    ]
    for shape in ((2, 7), (3, 2), (7, 2, 3), (7, 5, 3), (2, 3, 3), (2, 3), (2, 2), (4,), (2, 2), (2, 3)):
        scratch += [dma(shape), dma(shape)]
    return pl.pallas_call(
        kernel,
        name="meta_gradient",
        out_shape=jax.ShapeDtypeStruct((2, T, DH), BF),
        in_specs=[hbm] * 7 + [pl.BlockSpec(memory_space=pltpu.SMEM)],
        out_specs=pl.BlockSpec(memory_space=pltpu.VMEM),
        scratch_shapes=scratch,
        compiler_params=pltpu.CompilerParams(
            collective_id=0, has_side_effects=True, vmem_limit_bytes=60 * 2**20
        ),
    )(
        inputs,
        probe,
        address,
        payload,
        checkpoints.reshape(2, 3, 4, F),
        out_grad,
        adjoint.reshape(3, 4, F),
        inner_rate,
    )


def solution(mesh):
    split = Mesh(mesh.devices.reshape(NZ, NY, NX, NC), AXES)
    tok, head = ("z", "y"), ("x", "c")
    placed = (
        P(None, tok, head),
        P(None, head),
        P(None, head),
        P(None, head),
        P(None, None, head, tok, None),
        P(None, tok, head),
        P(None, head, tok, None),
        P(head),
    )
    return jax.shard_map(
        local, mesh=split, in_specs=placed, out_specs=P(None, tok, head), check_vma=False
    )
```

```python
import jax
import jax.numpy as jnp
from jax import lax
from jax.experimental import pallas as pl
from jax.experimental.pallas import tpu as pltpu
from jax.sharding import Mesh
from jax.sharding import PartitionSpec as P

AXES = ("z", "y", "x", "c")
NZ, NY, NX, NC = 16, 4, 4, 2
MESH = pl.DeviceIdType.MESH
BF = jnp.bfloat16
F32 = jnp.float32
T = 256
DH = 256
F = 512
D = 2048
W_LATE, B_LATE, W_EARLY, B_EARLY = 0, 1, 2, 3
SPLIT = (3, 3, 3, 4)


def mm(a, b):
    return jnp.dot(a, b, preferred_element_type=F32)


def mm_t(a, b):
    return lax.dot_general(a, b, (((1,), (1,)), ((), ())), preferred_element_type=F32)


def permutation():
    row = lax.broadcasted_iota(jnp.int32, (DH, DH), 0)
    place = lax.broadcasted_iota(jnp.int32, (DH, DH), 1)
    held = 64 * ((place // 4) % 4) + 16 * ((place // 16) % 4) + 4 * (place // 64) + place % 4
    return jnp.where(row == held, 1.0, 0.0).astype(BF)


def kernel(
    xin, pq, pk, pv, ck, og, adj, rate, out,
    xg, pr, pc, pp, gath, fb, adjv, tile, ogv, qkv, o_s, fw, hb, own, rsend,
    turned, r1, acc, sd, r2, part, fsend, rf, gcat, gp, back, base, pb, ro,
    ls, xs, xr, fs, fr, as_, ar, bs, br, r1s, r1r, r2s, r2r, rfs, rfr, cs, cr, ps, pr_, hs, hr,
):
    z, y = lax.axis_index("z"), lax.axis_index("y")
    x, c = lax.axis_index("x"), lax.axis_index("c")

    def dev(dz=0, dy=0, dx=0, dc=0):
        return (
            lax.rem(z + dz + NZ, NZ), lax.rem(y + dy, NY), lax.rem(x + dx, NX), lax.rem(c + dc, NC)
        )

    zh, zl = z // 4, lax.rem(z, 4)
    odd, pair_row = lax.rem(zh, 2), zh // 2
    flip = 4 - 8 * odd
    skip = 4 * c - 2
    near = [skip, 1, -1]

    barrier = pltpu.get_barrier_semaphore()
    partners = [dev(dz=d) for d in (4, -4, 2, -2, 1, -1)]
    partners += [dev(dy=d) for d in (1, 2, 3)] + [dev(dx=d) for d in (1, 2, 3)] + [dev(dc=1)]
    for partner in partners:
        pl.semaphore_signal(barrier, inc=1, device_id=partner, device_id_type=MESH)

    started = []

    def send(src, dst, ssem, rsem, device):
        copy = pltpu.make_async_remote_copy(
            src_ref=src, dst_ref=dst, send_sem=ssem, recv_sem=rsem,
            device_id=device, device_id_type=MESH,
        )
        copy.start()
        started.append(copy)
        return copy

    column = pl.multiple_of((x * 2 + c) * DH, DH)
    loads = [
        pltpu.make_async_copy(src, dst, ls.at[i])
        for i, (src, dst) in enumerate((
            (ck.at[1], fb.at[W_LATE, odd]),
            (adj, adjv),
            (ck.at[0], fb.at[W_EARLY, odd]),
            (xin.at[1], xg.at[1, :, pl.ds(column, DH)]),
            (pq, pr.at[0]),
            (pk, pr.at[1]),
            (pv, pr.at[2]),
            (og, ogv),
            (xin.at[0], xg.at[0, :, pl.ds(column, DH)]),
        ))
    ]
    for load in loads:
        load.start()
    pl.semaphore_wait(barrier, len(partners))

    far_one, far_two = {}, {}

    def far_send(s, piece):
        far_one[s] = send(piece, fb.at[s, odd], fs.at[s, 0], fr.at[s, 0], dev(dz=flip))

    x_copies = {}

    def x_send(s):
        block = xg.at[s, :, pl.ds(column, DH)]
        x_copies[s] = [
            send(xin.at[s], block, xs.at[s, i], xr.at[s, i], dev(dx=d)) for i, d in enumerate((2, 1, 3))
        ]
        x_copies[s].append(send(xin.at[s], block, xs.at[s, 3], xr.at[s, 3], dev(dc=1)))

    far_send(W_LATE, ck.at[1])
    loads[1].wait()
    fb[B_LATE, odd] = adjv[...].astype(BF)
    far_send(B_LATE, fb.at[B_LATE, odd])
    x_send(1)
    for i in (0, 2, 3):
        loads[i].wait()

    order = permutation()
    for i in range(3):
        loads[4 + i].wait()
        for j in range(8):
            rows = pl.ds(j * DH, DH)
            pc[rows, pl.ds(i * DH, DH)] = mm(pr[i, rows, :], order).astype(BF)

    def rows8(of):
        return pl.ds(pl.multiple_of(8 * of, 8), 8)

    def assemble(s):
        far_one[s].wait_recv()
        for m in range(3):
            for k in range(2):
                tile[m, pl.ds(4 * k, 4), :] = fb[s, k, m].astype(F32)
        for half in range(2):
            rows = tile[:, :, pl.ds(half * 256, 256)].astype(BF)
            for k in range(2):

                @pl.when(pair_row == k)
                def _():
                    gath[s, pl.ds(3 * half, 3), y, zl, pl.ds(8 * k, 8), :] = rows

        block = gath.at[s, :, y, zl, rows8(pair_row), :]
        far_two[s] = send(block, block, fs.at[s, 1], fr.at[s, 1], dev(dz=-flip))

    other = 1 - c
    first, last = {}, {}

    def to_near(block, ssem, rsem):
        return [send(block, block, ssem.at[i], rsem.at[i], dev(dz=d)) for i, d in enumerate(near)]

    def to_y(block, ssem, rsem):
        return [send(block, block, ssem.at[i], rsem.at[i], dev(dy=d)) for i, d in enumerate((2, 1, 3))]

    def gather_first(s):
        if s != B_EARLY:
            far_two[s].wait_recv()
        a, b = pl.ds(0, SPLIT[s]), pl.ds(SPLIT[s], 6 - SPLIT[s])
        first[s] = to_near(gath.at[s, a, y, zl], as_.at[s, 0], ar.at[s, 0])
        first[s] += to_y(gath.at[s, b, y, zl], as_.at[s, 1], ar.at[s, 1])

    def gather_last(s):
        for copy in first[s]:
            copy.wait_recv()
        a, b = pl.ds(0, SPLIT[s]), pl.ds(SPLIT[s], 6 - SPLIT[s])
        last[s] = to_y(gath.at[s, a, y], bs.at[s, 0], br.at[s, 0])
        last[s] += to_near(gath.at[s, b, :, zl], bs.at[s, 1], br.at[s, 1])

    def gather_end(s):
        for copy in last[s]:
            copy.wait_recv()

    relays = {}

    def x_relay(s):
        relays[s] = []
        for i, d in enumerate((2, 1, 3)):
            x_copies[s][i].wait_recv()
            source = pl.multiple_of((lax.rem(x + 4 - d, NX) * 2 + c) * DH, DH)
            block = xg.at[s, :, pl.ds(source, DH)]
            relays[s].append(send(block, block, xs.at[s, 4 + i], xr.at[s, 4 + i], dev(dc=1)))

    def project(s):
        for copy in [x_copies[s][3]] + relays[s]:
            copy.wait_recv()
        for i in range(3):
            qkv[s, i] = mm(xg[s], pc[:, pl.ds(i * DH, DH)]).astype(BF)

    factor = rate[0] / 16384.0

    def weight(s, half, m):
        return gath[s, 3 * half + m].reshape(DH, 256)

    def ahead(rows, s, m, to):
        for half in range(2):
            fw[to[0], to[1], :, pl.ds(half * 256, 256)] = mm(rows, weight(s, half, m))

    def behind(s, i, w, m):
        return mm_t(hb[s, i, :, pl.ds(0, 256)], weight(w, 0, m)) + mm_t(
            hb[s, i, :, pl.ds(256, 256)], weight(w, 1, m)
        )

    def forward(s, w):
        q, k, v = qkv[s, 0], qkv[s, 1], qkv[s, 2]
        ahead(q, w, 0, (s, 0))
        ahead(q, w, 1, (s, 1))
        ahead(o_s[s], w, 2, (s, 2))
        ahead(k, w, 0, (s, 3))
        ahead(k, w, 1, (s, 4))
        ahead(v, w, 2, (s, 5))

        @pl.loop(0, T // 16)
        def _(step):
            rows = pl.ds(pl.multiple_of(step * 16, 16), 16)
            gate, lift, back = fw[s, 0, rows, :], fw[s, 1, rows, :], fw[s, 2, rows, :]
            g = jax.nn.sigmoid(gate)
            act = gate * g
            if s > 0:
                hb[s, 0, rows, :] = (act * lift).astype(BF)
            hb[s, 1, rows, :] = (back * lift * (g * (1.0 + gate * (1.0 - g)))).astype(BF)
            hb[s, 2, rows, :] = (back * act).astype(BF)
            gate, u, e = fw[s, 3, rows, :], fw[s, 4, rows, :], fw[s, 5, rows, :]
            g = jax.nn.sigmoid(gate)
            act = factor * gate * g
            slope = factor * (g * (1.0 + gate * (1.0 - g)))
            bend = factor * (g * (1.0 - g) * (2.0 + gate * (1.0 - 2.0 * g)))
            us = u * slope
            fw[s, 0, rows, :] = us
            fw[s, 1, rows, :] = e * u * bend
            fw[s, 2, rows, :] = e * slope
            fw[s, 3, rows, :] = act
            hb[s, 6, rows, :] = (act * u).astype(BF)
            hb[s, 7, rows, :] = (e * us).astype(BF)
            hb[s, 8, rows, :] = (e * act).astype(BF)

    def sides(s, b, m):
        ahead(qkv[s, 1] if m < 2 else qkv[s, 2], b, m, (s, (7, 8, 6)[m]))

    def second(s):
        @pl.loop(0, T // 16)
        def _(step):
            rows = pl.ds(pl.multiple_of(step * 16, 16), 16)
            pull, one, three = fw[s, 6, rows, :], fw[s, 7, rows, :], fw[s, 8, rows, :]
            us, eub, es, act = (fw[s, i, rows, :] for i in range(4))
            hb[s, 3, rows, :] = (us * pull + one * eub + three * es).astype(BF)
            hb[s, 4, rows, :] = (act * pull + one * es).astype(BF)
            hb[s, 5, rows, :] = (one * us + three * act).astype(BF)

    def back_queries(s, w):
        grad = behind(s, 1, w, 0) + behind(s, 2, w, 1)
        gcat[s, :, pl.ds(0, DH)] = grad.astype(BF)

    def back_sides(s, b):
        back[0] = behind(s, 7, b, 0) + behind(s, 8, b, 1)
        back[1] = behind(s, 6, b, 2)

    def back_rest(s, w):
        grad = behind(s, 3, w, 0) + behind(s, 4, w, 1) + back[0]
        gcat[s, :, pl.ds(DH, DH)] = grad.astype(BF)
        grad = behind(s, 5, w, 2) + back[1]
        gcat[s, :, pl.ds(2 * DH, DH)] = grad.astype(BF)

    pair = {}
    query_part, rest_part = pl.ds(0, DH), pl.ds(DH, 2 * DH)

    def exchange(s, i, lanes):
        pair[s, i] = send(
            gcat.at[s, :, lanes], gp.at[s, :, lanes], ps.at[s, i], pr_.at[s, i], dev(dc=1)
        )

    heads = {}
    steps = (2, 1, 3, 0)

    def own_term(s, step, lanes):
        rows = pl.multiple_of((lax.rem(x + step, NX) * 2 + c) * DH, DH)
        return mm_t(gcat[s, :, lanes], pc[pl.ds(rows, DH), lanes])

    def pair_term(s, step, lanes):
        return mm_t(gp[s, :, lanes], pp[lax.rem(x + step, NX), :, lanes])

    def heads_queries(s):
        pair[s, 0].wait_recv()
        for i, step in enumerate(steps):
            base[i] = own_term(s, step, query_part) + pair_term(s, step, query_part)

    def heads_send(s):
        for i, step in enumerate(steps):
            base[i] = base[i] + own_term(s, step, rest_part)
        pair[s, 1].wait_recv()
        heads[s] = []
        for i, step in enumerate(steps[:3]):
            pb[s, i] = (base[i] + pair_term(s, step, rest_part)).astype(BF)
            heads[s].append(
                send(pb.at[s, i], ro.at[s, i], hs.at[s, i], hr.at[s, i], dev(dx=step))
            )
        base[3] = base[3] + pair_term(s, 0, rest_part)

    def heads_end(s):
        total = base[3]
        for i in range(3):
            heads[s][i].wait_recv()
            total = total + ro[s, i].astype(F32)
        out[s] = total.astype(BF)

    assemble(W_LATE)
    assemble(B_LATE)
    far_send(W_EARLY, ck.at[0])
    x_send(0)
    pc_copies = []
    for i in range(4):
        rows = pl.multiple_of((i * 2 + other) * DH, DH)
        pc_copies.append(
            send(pc.at[pl.ds(rows, DH), :], pp.at[i], cs.at[i], cr.at[i], dev(dc=1))
        )
    loads[7].wait()
    for s in range(2):
        o_s[s] = mm(ogv[s], order).astype(BF)
    x_relay(1)
    gather_first(W_LATE)
    gather_first(B_LATE)
    assemble(W_EARLY)
    project(1)
    gather_last(W_LATE)
    gather_last(B_LATE)
    gather_first(W_EARLY)
    for i, rows in enumerate((qkv[1, 1], qkv[1, 0], qkv[1, 2], o_s[1])):
        turned[i] = rows.T
    x_relay(0)
    loads[8].wait()
    project(0)
    gather_end(W_LATE)
    gather_last(W_EARLY)
    forward(1, W_LATE)
    back_queries(1, W_LATE)
    gather_end(B_LATE)
    for m in range(3):
        sides(1, B_LATE, m)
    second(1)

    terms = ((0, 3, 1, 1), (0, 4, 1, 2), (2, 5, 3, 0))
    split = SPLIT[B_EARLY]
    sums = {}
    for m, (left, i, right, j) in enumerate(terms):
        for half in range(2):
            lanes = pl.ds(half * 256, 256)
            h = 3 * half + m
            grad = mm(turned[left], hb[1, i, :, lanes]) + mm(turned[right], hb[1, j, :, lanes])
            grad = grad.reshape(4, 4, 16, 256)
            own[h] = grad
            rsend[h] = grad.astype(BF)
            if h < split:
                sums[h] = [
                    send(rsend.at[h, lax.rem(y + d, NY)], r1.at[h, n],
                         r1s.at[h, n], r1r.at[h, n], dev(dy=d))
                    for n, d in enumerate((2, 1, 3))
                ]
            else:
                sums[h] = [
                    send(rsend.at[h, :, lax.rem(z + d + NZ, 4)], r1.at[h, n],
                         r1s.at[h, n], r1r.at[h, n], dev(dz=d))
                    for n, d in enumerate(near)
                ]

    exchange(1, 0, query_part)
    back_sides(1, B_LATE)
    back_rest(1, W_LATE)
    exchange(1, 1, rest_part)

    def first_sum(h):
        for copy in sums[h]:
            copy.wait_recv()
        total = own[h, y] if h < split else own[h, :, zl]
        for i in range(3):
            total = total + r1[h, i].astype(F32)
        acc[h] = total
        sd[h] = total.astype(BF)

    a, b = pl.ds(0, split), pl.ds(split, 6 - split)
    for h in range(split):
        first_sum(h)
    two_a = [
        send(sd.at[a, lax.rem(z + d + NZ, 4)], r2.at[n, a], r2s.at[0, n], r2r.at[0, n], dev(dz=d))
        for n, d in enumerate(near)
    ]
    for h in range(split, 6):
        first_sum(h)
    two_b = [
        send(sd.at[b, lax.rem(y + d, NY)], r2.at[n, b], r2s.at[1, n], r2r.at[1, n], dev(dy=d))
        for n, d in enumerate((2, 1, 3))
    ]

    third = {}

    def far_sum(half, step):
        fsend[half, step] = part[pl.ds(3 * half, 3)].astype(BF)
        way = flip if half == step else -flip
        third[half] = send(
            fsend.at[half, step], rf.at[half, step], rfs.at[half, step], rfr.at[half, step], dev(dz=way)
        )

    for half, copies, place, span_of in ((0, two_a, zl, range(split)), (1, two_b, y, range(split, 6))):
        for copy in copies:
            copy.wait_recv()
        for h in span_of:
            total = acc[h, place]
            for i in range(3):
                total = total + r2[i, h].astype(F32)
            part[h] = total
            for k in range(4):
                mine = jnp.where(zh == k, 1.0, 0.0)
                rows = pl.ds(4 * k, 4)
                part[h, rows, :] = (
                    part[h, rows, :] + mine * adjv[h % 3, :, pl.ds(h // 3 * 256, 256)]
                )
        far_sum(half, 0)

    gather_end(W_EARLY)
    forward(0, W_EARLY)

    for half in range(2):
        third[half].wait_recv()
        part[pl.ds(3 * half, 3)] = part[pl.ds(3 * half, 3)] + rf[half, 0].astype(F32)
        far_sum(half, 1)

    for copy in pc_copies:
        copy.wait_recv()
    back_queries(0, W_EARLY)
    exchange(0, 0, query_part)
    heads_queries(1)
    heads_send(1)

    for half in range(2):
        third[half].wait_recv()
        total = part[pl.ds(3 * half, 3)] + rf[half, 1].astype(F32)
        gath[B_EARLY, pl.ds(3 * half, 3), y, zl] = total.astype(BF)
    gather_first(B_EARLY)
    gather_last(B_EARLY)
    heads_end(1)
    heads_queries(0)
    gather_end(B_EARLY)
    for m in range(3):
        sides(0, B_EARLY, m)

    second(0)
    back_sides(0, B_EARLY)
    back_rest(0, W_EARLY)
    exchange(0, 1, rest_part)
    heads_send(0)
    heads_end(0)

    for copy in started:
        copy.wait_send()


def local(inputs, probe, address, payload, checkpoints, out_grad, adjoint, inner_rate):
    hbm = pl.BlockSpec(memory_space=pl.ANY)
    dma = pltpu.SemaphoreType.DMA
    scratch = [
        pltpu.VMEM((2, T, D), BF),
        pltpu.VMEM((3, D, DH), BF),
        pltpu.VMEM((D, 3 * DH), BF),
        pltpu.VMEM((4, DH, 3 * DH), BF),
        pltpu.VMEM((4, 6, 4, 4, 16, 256), BF),
        pltpu.VMEM((3, 2, 3, 4, F), BF),
        pltpu.VMEM((3, 4, F), F32),
        pltpu.VMEM((3, 8, F), F32),
        pltpu.VMEM((2, T, DH), BF),
        pltpu.VMEM((2, 3, T, DH), BF),
        pltpu.VMEM((2, T, DH), BF),
        pltpu.VMEM((2, 9, T, F), F32),
        pltpu.VMEM((2, 9, T, F), BF),
        pltpu.VMEM((6, 4, 4, 16, 256), F32),
        pltpu.VMEM((6, 4, 4, 16, 256), BF),
        pltpu.VMEM((4, DH, T), BF),
        pltpu.VMEM((6, 3, 4, 16, 256), BF),
        pltpu.VMEM((6, 4, 16, 256), F32),
        pltpu.VMEM((6, 4, 16, 256), BF),
        pltpu.VMEM((3, 6, 16, 256), BF),
        pltpu.VMEM((6, 16, 256), F32),
        pltpu.VMEM((2, 2, 3, 16, 256), BF),
        pltpu.VMEM((2, 2, 3, 16, 256), BF),
        pltpu.VMEM((2, T, 3 * DH), BF),
        pltpu.VMEM((2, T, 3 * DH), BF),
        pltpu.VMEM((2, T, DH), F32),
        pltpu.VMEM((4, T, DH), F32),
        pltpu.VMEM((2, 3, T, DH), BF),
        pltpu.VMEM((2, 3, T, DH), BF),
        dma((9,)),
    ]
    for shape in ((2, 7), (3, 2), (4, 2, 3), (4, 2, 3), (6, 3), (2, 3), (2, 2), (4,), (2, 2), (2, 3)):
        scratch += [dma(shape), dma(shape)]
    return pl.pallas_call(
        kernel,
        name="meta_gradient",
        out_shape=jax.ShapeDtypeStruct((2, T, DH), BF),
        in_specs=[hbm] * 7 + [pl.BlockSpec(memory_space=pltpu.SMEM)],
        out_specs=pl.BlockSpec(memory_space=pltpu.VMEM),
        scratch_shapes=scratch,
        compiler_params=pltpu.CompilerParams(
            collective_id=0, has_side_effects=True, vmem_limit_bytes=60 * 2**20
        ),
    )(
        inputs,
        probe,
        address,
        payload,
        checkpoints.reshape(2, 3, 4, F),
        out_grad,
        adjoint.reshape(3, 4, F),
        inner_rate,
    )


def solution(mesh):
    split = Mesh(mesh.devices.reshape(NZ, NY, NX, NC), AXES)
    tok, head = ("z", "y"), ("x", "c")
    placed = (
        P(None, tok, head),
        P(None, head),
        P(None, head),
        P(None, head),
        P(None, None, head, tok, None),
        P(None, tok, head),
        P(None, head, tok, None),
        P(head),
    )
    return jax.shard_map(
        local, mesh=split, in_specs=placed, out_specs=P(None, tok, head), check_vma=False
    )
```

```python
import jax
import jax.numpy as jnp
from jax import lax
from jax.experimental import pallas as pl
from jax.experimental.pallas import tpu as pltpu
from jax.sharding import Mesh
from jax.sharding import PartitionSpec as P

AXES = ("z", "y", "x", "c")
NZ, NY, NX, NC = 16, 4, 4, 2
MESH = pl.DeviceIdType.MESH
BF = jnp.bfloat16
F32 = jnp.float32
T = 256
DH = 256
F = 512
D = 2048
W_LATE, B_LATE, W_EARLY, B_EARLY = 0, 1, 2, 3
SPLIT = (3, 3, 6, 3)


def mm(a, b):
    return jnp.dot(a, b, preferred_element_type=F32)


def mm_t(a, b):
    return lax.dot_general(a, b, (((1,), (1,)), ((), ())), preferred_element_type=F32)


def permutation():
    row = lax.broadcasted_iota(jnp.int32, (DH, DH), 0)
    place = lax.broadcasted_iota(jnp.int32, (DH, DH), 1)
    held = 64 * ((place // 4) % 4) + 16 * ((place // 16) % 4) + 4 * (place // 64) + place % 4
    return jnp.where(row == held, 1.0, 0.0).astype(BF)


def kernel(
    xin, pq, pk, pv, ck, og, adj, rate, out,
    xg, pr, pc, pp, gath, fb, adjv, tile, ogv, qkv, o_s, fw, hb, own, rsend,
    turned, r1, acc, sd, r2, part, fsend, rf, gcat, gp, back, base, pb, ro,
    ls, xs, xr, fs, fr, as_, ar, bs, br, r1s, r1r, r2s, r2r, rfs, rfr, cs, cr, ps, pr_, hs, hr,
):
    z, y = lax.axis_index("z"), lax.axis_index("y")
    x, c = lax.axis_index("x"), lax.axis_index("c")

    def dev(dz=0, dy=0, dx=0, dc=0):
        return (
            lax.rem(z + dz + NZ, NZ), lax.rem(y + dy, NY), lax.rem(x + dx, NX), lax.rem(c + dc, NC)
        )

    zh, zl = z // 4, lax.rem(z, 4)
    odd, pair_row = lax.rem(zh, 2), zh // 2
    flip = 4 - 8 * odd
    skip = 4 * c - 2
    near = [skip, 1, -1]

    barrier = pltpu.get_barrier_semaphore()
    partners = [dev(dz=d) for d in (4, -4, 2, -2, 1, -1)]
    partners += [dev(dy=d) for d in (1, 2, 3)] + [dev(dx=d) for d in (1, 2, 3)] + [dev(dc=1)]
    for partner in partners:
        pl.semaphore_signal(barrier, inc=1, device_id=partner, device_id_type=MESH)

    started = []

    def send(src, dst, ssem, rsem, device):
        copy = pltpu.make_async_remote_copy(
            src_ref=src, dst_ref=dst, send_sem=ssem, recv_sem=rsem,
            device_id=device, device_id_type=MESH,
        )
        copy.start()
        started.append(copy)
        return copy

    column = pl.multiple_of((x * 2 + c) * DH, DH)
    loads = [
        pltpu.make_async_copy(src, dst, ls.at[i])
        for i, (src, dst) in enumerate((
            (ck.at[1], fb.at[W_LATE, odd]),
            (adj, adjv),
            (ck.at[0], fb.at[W_EARLY, odd]),
            (xin.at[1], xg.at[1, :, pl.ds(column, DH)]),
            (pq, pr.at[0]),
            (pk, pr.at[1]),
            (pv, pr.at[2]),
            (og, ogv),
            (xin.at[0], xg.at[0, :, pl.ds(column, DH)]),
        ))
    ]
    for load in loads:
        load.start()
    pl.semaphore_wait(barrier, len(partners))

    far_one, far_two = {}, {}

    def far_send(s, piece):
        far_one[s] = send(piece, fb.at[s, odd], fs.at[s, 0], fr.at[s, 0], dev(dz=flip))

    x_copies = {}

    def x_send(s):
        block = xg.at[s, :, pl.ds(column, DH)]
        x_copies[s] = [
            send(xin.at[s], block, xs.at[s, i], xr.at[s, i], dev(dx=d)) for i, d in enumerate((2, 1, 3))
        ]
        x_copies[s].append(send(xin.at[s], block, xs.at[s, 3], xr.at[s, 3], dev(dc=1)))

    far_send(W_LATE, ck.at[1])
    loads[1].wait()
    fb[B_LATE, odd] = adjv[...].astype(BF)
    far_send(B_LATE, fb.at[B_LATE, odd])
    x_send(1)
    for i in (0, 2, 3):
        loads[i].wait()

    order = permutation()
    for i in range(3):
        loads[4 + i].wait()
        for j in range(8):
            rows = pl.ds(j * DH, DH)
            pc[rows, pl.ds(i * DH, DH)] = mm(pr[i, rows, :], order).astype(BF)

    def rows8(of):
        return pl.ds(pl.multiple_of(8 * of, 8), 8)

    def assemble(s):
        far_one[s].wait_recv()
        for m in range(3):
            for k in range(2):
                tile[m, pl.ds(4 * k, 4), :] = fb[s, k, m].astype(F32)
        for half in range(2):
            rows = tile[:, :, pl.ds(half * 256, 256)].astype(BF)
            for k in range(2):

                @pl.when(pair_row == k)
                def _():
                    gath[s, pl.ds(3 * half, 3), y, zl, pl.ds(8 * k, 8), :] = rows

        block = gath.at[s, :, y, zl, rows8(pair_row), :]
        far_two[s] = send(block, block, fs.at[s, 1], fr.at[s, 1], dev(dz=-flip))

    other = 1 - c
    first, last = {}, {}

    def to_near(block, ssem, rsem):
        return [send(block, block, ssem.at[i], rsem.at[i], dev(dz=d)) for i, d in enumerate(near)]

    def to_y(block, ssem, rsem):
        return [send(block, block, ssem.at[i], rsem.at[i], dev(dy=d)) for i, d in enumerate((2, 1, 3))]

    def gather_first(s):
        if s != B_EARLY:
            far_two[s].wait_recv()
        a, b = pl.ds(0, SPLIT[s]), pl.ds(SPLIT[s], 6 - SPLIT[s])
        first[s] = to_near(gath.at[s, a, y, zl], as_.at[s, 0], ar.at[s, 0])
        if SPLIT[s] < 6:
            first[s] += to_y(gath.at[s, b, y, zl], as_.at[s, 1], ar.at[s, 1])

    def gather_last(s):
        for copy in first[s]:
            copy.wait_recv()
        a, b = pl.ds(0, SPLIT[s]), pl.ds(SPLIT[s], 6 - SPLIT[s])
        last[s] = to_y(gath.at[s, a, y], bs.at[s, 0], br.at[s, 0])
        if SPLIT[s] < 6:
            last[s] += to_near(gath.at[s, b, :, zl], bs.at[s, 1], br.at[s, 1])

    def gather_end(s):
        for copy in last[s]:
            copy.wait_recv()

    relays = {}

    def x_relay(s):
        relays[s] = []
        for i, d in enumerate((2, 1, 3)):
            x_copies[s][i].wait_recv()
            source = pl.multiple_of((lax.rem(x + 4 - d, NX) * 2 + c) * DH, DH)
            block = xg.at[s, :, pl.ds(source, DH)]
            relays[s].append(send(block, block, xs.at[s, 4 + i], xr.at[s, 4 + i], dev(dc=1)))

    def project(s):
        for copy in [x_copies[s][3]] + relays[s]:
            copy.wait_recv()
        for i in range(3):
            qkv[s, i] = mm(xg[s], pc[:, pl.ds(i * DH, DH)]).astype(BF)

    factor = rate[0] / 16384.0

    def weight(s, half, m):
        return gath[s, 3 * half + m].reshape(DH, 256)

    def ahead(rows, s, m, to):
        for half in range(2):
            fw[to[0], to[1], :, pl.ds(half * 256, 256)] = mm(rows, weight(s, half, m))

    def behind(s, i, w, m):
        return mm_t(hb[s, i, :, pl.ds(0, 256)], weight(w, 0, m)) + mm_t(
            hb[s, i, :, pl.ds(256, 256)], weight(w, 1, m)
        )

    def forward(s, w):
        q, k, v = qkv[s, 0], qkv[s, 1], qkv[s, 2]
        ahead(q, w, 0, (s, 0))
        ahead(q, w, 1, (s, 1))
        ahead(o_s[s], w, 2, (s, 2))
        ahead(k, w, 0, (s, 3))
        ahead(k, w, 1, (s, 4))
        ahead(v, w, 2, (s, 5))

        @pl.loop(0, T // 16)
        def _(step):
            rows = pl.ds(pl.multiple_of(step * 16, 16), 16)
            gate, lift, back = fw[s, 0, rows, :], fw[s, 1, rows, :], fw[s, 2, rows, :]
            g = jax.nn.sigmoid(gate)
            act = gate * g
            if s > 0:
                hb[s, 0, rows, :] = (act * lift).astype(BF)
            hb[s, 1, rows, :] = (back * lift * (g * (1.0 + gate * (1.0 - g)))).astype(BF)
            hb[s, 2, rows, :] = (back * act).astype(BF)
            gate, u, e = fw[s, 3, rows, :], fw[s, 4, rows, :], fw[s, 5, rows, :]
            g = jax.nn.sigmoid(gate)
            act = factor * gate * g
            slope = factor * (g * (1.0 + gate * (1.0 - g)))
            bend = factor * (g * (1.0 - g) * (2.0 + gate * (1.0 - 2.0 * g)))
            us = u * slope
            fw[s, 0, rows, :] = us
            fw[s, 1, rows, :] = e * u * bend
            fw[s, 2, rows, :] = e * slope
            fw[s, 3, rows, :] = act
            hb[s, 6, rows, :] = (act * u).astype(BF)
            hb[s, 7, rows, :] = (e * us).astype(BF)
            hb[s, 8, rows, :] = (e * act).astype(BF)

    def sides(s, b, m):
        ahead(qkv[s, 1] if m < 2 else qkv[s, 2], b, m, (s, (7, 8, 6)[m]))

    def second(s):
        @pl.loop(0, T // 16)
        def _(step):
            rows = pl.ds(pl.multiple_of(step * 16, 16), 16)
            pull, one, three = fw[s, 6, rows, :], fw[s, 7, rows, :], fw[s, 8, rows, :]
            us, eub, es, act = (fw[s, i, rows, :] for i in range(4))
            hb[s, 3, rows, :] = (us * pull + one * eub + three * es).astype(BF)
            hb[s, 4, rows, :] = (act * pull + one * es).astype(BF)
            hb[s, 5, rows, :] = (one * us + three * act).astype(BF)

    def back_queries(s, w):
        grad = behind(s, 1, w, 0) + behind(s, 2, w, 1)
        gcat[s, :, pl.ds(0, DH)] = grad.astype(BF)

    def back_sides(s, b):
        back[0] = behind(s, 7, b, 0) + behind(s, 8, b, 1)
        back[1] = behind(s, 6, b, 2)

    def back_rest(s, w):
        grad = behind(s, 3, w, 0) + behind(s, 4, w, 1) + back[0]
        gcat[s, :, pl.ds(DH, DH)] = grad.astype(BF)
        grad = behind(s, 5, w, 2) + back[1]
        gcat[s, :, pl.ds(2 * DH, DH)] = grad.astype(BF)

    pair = {}
    query_part, rest_part = pl.ds(0, DH), pl.ds(DH, 2 * DH)

    def exchange(s, i, lanes):
        pair[s, i] = send(
            gcat.at[s, :, lanes], gp.at[s, :, lanes], ps.at[s, i], pr_.at[s, i], dev(dc=1)
        )

    heads = {}
    steps = (2, 1, 3, 0)

    def own_term(s, step, lanes):
        rows = pl.multiple_of((lax.rem(x + step, NX) * 2 + c) * DH, DH)
        return mm_t(gcat[s, :, lanes], pc[pl.ds(rows, DH), lanes])

    def pair_term(s, step, lanes):
        return mm_t(gp[s, :, lanes], pp[lax.rem(x + step, NX), :, lanes])

    def heads_queries(s):
        pair[s, 0].wait_recv()
        for i, step in enumerate(steps):
            base[i] = own_term(s, step, query_part) + pair_term(s, step, query_part)

    def heads_send(s):
        for i, step in enumerate(steps):
            base[i] = base[i] + own_term(s, step, rest_part)
        pair[s, 1].wait_recv()
        heads[s] = []
        for i, step in enumerate(steps[:3]):
            pb[s, i] = (base[i] + pair_term(s, step, rest_part)).astype(BF)
            heads[s].append(
                send(pb.at[s, i], ro.at[s, i], hs.at[s, i], hr.at[s, i], dev(dx=step))
            )
        base[3] = base[3] + pair_term(s, 0, rest_part)

    def heads_end(s):
        total = base[3]
        for i in range(3):
            heads[s][i].wait_recv()
            total = total + ro[s, i].astype(F32)
        out[s] = total.astype(BF)

    assemble(W_LATE)
    assemble(B_LATE)
    far_send(W_EARLY, ck.at[0])
    x_send(0)
    pc_copies = []
    for i in range(4):
        rows = pl.multiple_of((i * 2 + other) * DH, DH)
        pc_copies.append(
            send(pc.at[pl.ds(rows, DH), :], pp.at[i], cs.at[i], cr.at[i], dev(dc=1))
        )
    loads[7].wait()
    for s in range(2):
        o_s[s] = mm(ogv[s], order).astype(BF)
    x_relay(1)
    gather_first(W_LATE)
    gather_first(B_LATE)
    project(1)
    gather_last(W_LATE)
    gather_last(B_LATE)
    assemble(W_EARLY)
    for i, rows in enumerate((qkv[1, 1], qkv[1, 0], qkv[1, 2], o_s[1])):
        turned[i] = rows.T
    gather_end(W_LATE)
    forward(1, W_LATE)
    back_queries(1, W_LATE)
    gather_first(W_EARLY)
    gather_end(B_LATE)
    for m in range(3):
        sides(1, B_LATE, m)
    second(1)

    terms = ((0, 3, 1, 1), (0, 4, 1, 2), (2, 5, 3, 0))
    split = SPLIT[B_EARLY]
    sums = {}
    for m, (left, i, right, j) in enumerate(terms):
        for half in range(2):
            lanes = pl.ds(half * 256, 256)
            h = 3 * half + m
            grad = mm(turned[left], hb[1, i, :, lanes]) + mm(turned[right], hb[1, j, :, lanes])
            grad = grad.reshape(4, 4, 16, 256)
            own[h] = grad
            rsend[h] = grad.astype(BF)
            if h < split:
                sums[h] = [
                    send(rsend.at[h, lax.rem(y + d, NY)], r1.at[h, n],
                         r1s.at[h, n], r1r.at[h, n], dev(dy=d))
                    for n, d in enumerate((2, 1, 3))
                ]
            else:
                sums[h] = [
                    send(rsend.at[h, :, lax.rem(z + d + NZ, 4)], r1.at[h, n],
                         r1s.at[h, n], r1r.at[h, n], dev(dz=d))
                    for n, d in enumerate(near)
                ]

    exchange(1, 0, query_part)
    back_sides(1, B_LATE)
    back_rest(1, W_LATE)
    exchange(1, 1, rest_part)
    x_relay(0)

    def first_sum(h):
        for copy in sums[h]:
            copy.wait_recv()
        total = own[h, y] if h < split else own[h, :, zl]
        for i in range(3):
            total = total + r1[h, i].astype(F32)
        acc[h] = total
        sd[h] = total.astype(BF)

    a, b = pl.ds(0, split), pl.ds(split, 6 - split)
    for h in range(split):
        first_sum(h)
    two_a = [
        send(sd.at[a, lax.rem(z + d + NZ, 4)], r2.at[n, a], r2s.at[0, n], r2r.at[0, n], dev(dz=d))
        for n, d in enumerate(near)
    ]
    for h in range(split, 6):
        first_sum(h)
    two_b = [
        send(sd.at[b, lax.rem(y + d, NY)], r2.at[n, b], r2s.at[1, n], r2r.at[1, n], dev(dy=d))
        for n, d in enumerate((2, 1, 3))
    ]

    loads[8].wait()
    project(0)

    third = {}

    def far_sum(half, step):
        fsend[half, step] = part[pl.ds(3 * half, 3)].astype(BF)
        way = flip if half == step else -flip
        third[half] = send(
            fsend.at[half, step], rf.at[half, step], rfs.at[half, step], rfr.at[half, step], dev(dz=way)
        )

    for half, copies, place, span_of in ((0, two_a, zl, range(split)), (1, two_b, y, range(split, 6))):
        for copy in copies:
            copy.wait_recv()
        for h in span_of:
            total = acc[h, place]
            for i in range(3):
                total = total + r2[i, h].astype(F32)
            part[h] = total
            for k in range(4):
                mine = jnp.where(zh == k, 1.0, 0.0)
                rows = pl.ds(4 * k, 4)
                part[h, rows, :] = (
                    part[h, rows, :] + mine * adjv[h % 3, :, pl.ds(h // 3 * 256, 256)]
                )
        far_sum(half, 0)

    gather_last(W_EARLY)
    for copy in pc_copies:
        copy.wait_recv()
    heads_queries(1)
    heads_send(1)

    for half in range(2):
        third[half].wait_recv()
        part[pl.ds(3 * half, 3)] = part[pl.ds(3 * half, 3)] + rf[half, 0].astype(F32)
        far_sum(half, 1)

    for half in range(2):
        third[half].wait_recv()
        total = part[pl.ds(3 * half, 3)] + rf[half, 1].astype(F32)
        gath[B_EARLY, pl.ds(3 * half, 3), y, zl] = total.astype(BF)
    gather_first(B_EARLY)
    gather_last(B_EARLY)
    heads_end(1)
    gather_end(W_EARLY)
    forward(0, W_EARLY)
    back_queries(0, W_EARLY)
    exchange(0, 0, query_part)
    heads_queries(0)
    gather_end(B_EARLY)
    for m in range(3):
        sides(0, B_EARLY, m)

    second(0)
    back_sides(0, B_EARLY)
    back_rest(0, W_EARLY)
    exchange(0, 1, rest_part)
    heads_send(0)
    heads_end(0)

    for copy in started:
        copy.wait_send()


def local(inputs, probe, address, payload, checkpoints, out_grad, adjoint, inner_rate):
    hbm = pl.BlockSpec(memory_space=pl.ANY)
    dma = pltpu.SemaphoreType.DMA
    scratch = [
        pltpu.VMEM((2, T, D), BF),
        pltpu.VMEM((3, D, DH), BF),
        pltpu.VMEM((D, 3 * DH), BF),
        pltpu.VMEM((4, DH, 3 * DH), BF),
        pltpu.VMEM((4, 6, 4, 4, 16, 256), BF),
        pltpu.VMEM((3, 2, 3, 4, F), BF),
        pltpu.VMEM((3, 4, F), F32),
        pltpu.VMEM((3, 8, F), F32),
        pltpu.VMEM((2, T, DH), BF),
        pltpu.VMEM((2, 3, T, DH), BF),
        pltpu.VMEM((2, T, DH), BF),
        pltpu.VMEM((2, 9, T, F), F32),
        pltpu.VMEM((2, 9, T, F), BF),
        pltpu.VMEM((6, 4, 4, 16, 256), F32),
        pltpu.VMEM((6, 4, 4, 16, 256), BF),
        pltpu.VMEM((4, DH, T), BF),
        pltpu.VMEM((6, 3, 4, 16, 256), BF),
        pltpu.VMEM((6, 4, 16, 256), F32),
        pltpu.VMEM((6, 4, 16, 256), BF),
        pltpu.VMEM((3, 6, 16, 256), BF),
        pltpu.VMEM((6, 16, 256), F32),
        pltpu.VMEM((2, 2, 3, 16, 256), BF),
        pltpu.VMEM((2, 2, 3, 16, 256), BF),
        pltpu.VMEM((2, T, 3 * DH), BF),
        pltpu.VMEM((2, T, 3 * DH), BF),
        pltpu.VMEM((2, T, DH), F32),
        pltpu.VMEM((4, T, DH), F32),
        pltpu.VMEM((2, 3, T, DH), BF),
        pltpu.VMEM((2, 3, T, DH), BF),
        dma((9,)),
    ]
    for shape in ((2, 7), (3, 2), (4, 2, 3), (4, 2, 3), (6, 3), (2, 3), (2, 2), (4,), (2, 2), (2, 3)):
        scratch += [dma(shape), dma(shape)]
    return pl.pallas_call(
        kernel,
        name="meta_gradient",
        out_shape=jax.ShapeDtypeStruct((2, T, DH), BF),
        in_specs=[hbm] * 7 + [pl.BlockSpec(memory_space=pltpu.SMEM)],
        out_specs=pl.BlockSpec(memory_space=pltpu.VMEM),
        scratch_shapes=scratch,
        compiler_params=pltpu.CompilerParams(
            collective_id=0, has_side_effects=True, vmem_limit_bytes=60 * 2**20
        ),
    )(
        inputs,
        probe,
        address,
        payload,
        checkpoints.reshape(2, 3, 4, F),
        out_grad,
        adjoint.reshape(3, 4, F),
        inner_rate,
    )


def solution(mesh):
    split = Mesh(mesh.devices.reshape(NZ, NY, NX, NC), AXES)
    tok, head = ("z", "y"), ("x", "c")
    placed = (
        P(None, tok, head),
        P(None, head),
        P(None, head),
        P(None, head),
        P(None, None, head, tok, None),
        P(None, tok, head),
        P(None, head, tok, None),
        P(head),
    )
    return jax.shard_map(
        local, mesh=split, in_specs=placed, out_specs=P(None, tok, head), check_vma=False
    )
```

```python
import jax
import jax.numpy as jnp
from jax import lax
from jax.experimental import pallas as pl
from jax.experimental.pallas import tpu as pltpu
from jax.sharding import Mesh
from jax.sharding import PartitionSpec as P

AXES = ("z", "y", "x", "c")
NZ, NY, NX, NC = 16, 4, 4, 2
MESH = pl.DeviceIdType.MESH
BF = jnp.bfloat16
F32 = jnp.float32
T = 256
DH = 256
F = 512
D = 2048
W_LATE, B_LATE, W_EARLY, B_EARLY = 0, 1, 2, 3


def mm(a, b):
    return jnp.dot(a, b, preferred_element_type=F32)


def mm_t(a, b):
    return lax.dot_general(a, b, (((1,), (1,)), ((), ())), preferred_element_type=F32)


def permutation():
    row = lax.broadcasted_iota(jnp.int32, (DH, DH), 0)
    place = lax.broadcasted_iota(jnp.int32, (DH, DH), 1)
    held = 64 * ((place // 4) % 4) + 16 * ((place // 16) % 4) + 4 * (place // 64) + place % 4
    return jnp.where(row == held, 1.0, 0.0).astype(BF)


def kernel(
    xin, pq, pk, pv, ck, og, adj, rate, out,
    xg, pr, pc, pp, gath, fb, adjv, tile, ogv, qkv, o_s, fw, hb, own, rsend,
    turned, r1, acc, sd, r2, part, fsend, rf, gcat, gp, back, base, pb, ro,
    ls, xs, xr, fs, fr, as_, ar, bs, br, r1s, r1r, r2s, r2r, rfs, rfr, cs, cr, ps, pr_, hs, hr,
):
    z, y = lax.axis_index("z"), lax.axis_index("y")
    x, c = lax.axis_index("x"), lax.axis_index("c")

    def dev(dz=0, dy=0, dx=0, dc=0):
        return (
            lax.rem(z + dz + NZ, NZ), lax.rem(y + dy, NY), lax.rem(x + dx, NX), lax.rem(c + dc, NC)
        )

    zh, zl = z // 4, lax.rem(z, 4)
    skip = 4 * c - 2
    near = [1, -1, skip]

    barrier = pltpu.get_barrier_semaphore()
    partners = [dev(dz=d) for d in (4, -4, 2, -2, 1, -1)]
    partners += [dev(dy=d) for d in (1, 2, 3)] + [dev(dx=d) for d in (1, 2, 3)] + [dev(dc=1)]
    for partner in partners:
        pl.semaphore_signal(barrier, inc=1, device_id=partner, device_id_type=MESH)

    started = []

    def send(src, dst, ssem, rsem, device):
        copy = pltpu.make_async_remote_copy(
            src_ref=src, dst_ref=dst, send_sem=ssem, recv_sem=rsem,
            device_id=device, device_id_type=MESH,
        )
        copy.start()
        started.append(copy)
        return copy

    column = pl.multiple_of((x * 2 + c) * DH, DH)
    loads = [
        pltpu.make_async_copy(src, dst, ls.at[i])
        for i, (src, dst) in enumerate((
            (ck.at[1], fb.at[W_LATE, zh]),
            (adj, adjv),
            (ck.at[0], fb.at[W_EARLY, zh]),
            (xin.at[1], xg.at[1, :, pl.ds(column, DH)]),
            (pq, pr.at[0]),
            (pk, pr.at[1]),
            (pv, pr.at[2]),
            (og, ogv),
            (xin.at[0], xg.at[0, :, pl.ds(column, DH)]),
        ))
    ]
    for load in loads:
        load.start()
    for load in loads[:4]:
        load.wait()
    fb[B_LATE, zh] = adjv[...].astype(BF)

    pl.semaphore_wait(barrier, len(partners))

    far_copies = {}

    def far_send(i, sets):
        piece = fb.at[sets, zh]
        far_copies[i] = [
            send(piece, piece, fs.at[i, n], fr.at[i, n], dev(dz=d)) for n, d in enumerate((4, -4))
        ]

    def far_relay(i, sets):
        for copy in far_copies[i]:
            copy.wait_recv()
        below = fb.at[sets, lax.rem(zh + 3, 4), pl.ds(0, 1)]
        above = fb.at[sets, lax.rem(zh + 1, 4), pl.ds(1, 2)]
        far_copies[i] = [
            send(below, below, fs.at[i, 2], fr.at[i, 2], dev(dz=4)),
            send(above, above, fs.at[i, 3], fr.at[i, 3], dev(dz=-4)),
        ]

    x_copies = {}

    def x_send(s):
        block = xg.at[s, :, pl.ds(column, DH)]
        x_copies[s] = [
            send(xin.at[s], block, xs.at[s, i], xr.at[s, i], dev(dx=d)) for i, d in enumerate((2, 1, 3))
        ]
        x_copies[s].append(send(xin.at[s], block, xs.at[s, 3], xr.at[s, 3], dev(dc=1)))

    late, early = pl.ds(0, 2), pl.ds(2, 1)
    far_send(0, late)
    x_send(1)
    far_send(1, early)
    x_send(0)

    order = permutation()
    for i in range(3):
        loads[4 + i].wait()
        for j in range(8):
            rows = pl.ds(j * DH, DH)
            pc[rows, pl.ds(i * DH, DH)] = mm(pr[i, rows, :], order).astype(BF)

    far_relay(0, late)
    far_relay(1, early)

    other = 1 - c
    pc_copies = []
    for i in range(4):
        rows = pl.multiple_of((i * 2 + other) * DH, DH)
        pc_copies.append(
            send(pc.at[pl.ds(rows, DH), :], pp.at[i], cs.at[i], cr.at[i], dev(dc=1))
        )
    loads[7].wait()
    for s in range(2):
        o_s[s] = mm(ogv[s], order).astype(BF)

    first, last = {}, {}

    def to_near(block, ssem, rsem):
        return [send(block, block, ssem.at[i], rsem.at[i], dev(dz=d)) for i, d in enumerate(near)]

    def to_y(block, ssem, rsem):
        return [send(block, block, ssem.at[i], rsem.at[i], dev(dy=d)) for i, d in enumerate((2, 1, 3))]

    def swapped(s, half):
        return half == 1 and s != W_EARLY

    def gather_first(s):
        first[s] = []
        for half in range(2):
            block = gath.at[s, half, :, y, zl]
            stage = to_y if swapped(s, half) else to_near
            first[s] += stage(block, as_.at[s, half], ar.at[s, half])

    def gather_last(s):
        for copy in first[s]:
            copy.wait_recv()
        last[s] = []
        for half in range(2):
            if swapped(s, half):
                last[s] += to_near(gath.at[s, half, :, :, zl], bs.at[s, half], br.at[s, half])
            else:
                last[s] += to_y(gath.at[s, half, :, y], bs.at[s, half], br.at[s, half])

    def gather_end(s):
        for copy in last[s]:
            copy.wait_recv()

    def far_end(i):
        for copy in far_copies[i]:
            copy.wait_recv()

    def assemble(s):
        for m in range(3):
            for k in range(4):
                tile[m, pl.ds(4 * k, 4), :] = fb[s, k, m].astype(F32)
            gath[s, 0, m, y, zl] = tile[m, :, pl.ds(0, 256)].astype(BF)
            gath[s, 1, m, y, zl] = tile[m, :, pl.ds(256, 256)].astype(BF)

    relays = {}

    def x_relay(s):
        relays[s] = []
        for i, d in enumerate((2, 1, 3)):
            x_copies[s][i].wait_recv()
            source = pl.multiple_of((lax.rem(x + 4 - d, NX) * 2 + c) * DH, DH)
            block = xg.at[s, :, pl.ds(source, DH)]
            relays[s].append(send(block, block, xs.at[s, 4 + i], xr.at[s, 4 + i], dev(dc=1)))

    def project(s):
        for copy in [x_copies[s][3]] + relays[s]:
            copy.wait_recv()
        for i in range(3):
            qkv[s, i] = mm(xg[s], pc[:, pl.ds(i * DH, DH)]).astype(BF)

    factor = rate[0] / 16384.0

    def weight(s, half, m):
        return gath[s, half, m].reshape(DH, 256)

    def ahead(rows, s, m, to):
        for half in range(2):
            fw[to[0], to[1], :, pl.ds(half * 256, 256)] = mm(rows, weight(s, half, m))

    def behind(s, i, w, m):
        return mm_t(hb[s, i, :, pl.ds(0, 256)], weight(w, 0, m)) + mm_t(
            hb[s, i, :, pl.ds(256, 256)], weight(w, 1, m)
        )

    def forward(s, w):
        q, k, v = qkv[s, 0], qkv[s, 1], qkv[s, 2]
        ahead(q, w, 0, (s, 0))
        ahead(q, w, 1, (s, 1))
        ahead(o_s[s], w, 2, (s, 2))
        ahead(k, w, 0, (s, 3))
        ahead(k, w, 1, (s, 4))
        ahead(v, w, 2, (s, 5))

        @pl.loop(0, T // 16)
        def _(step):
            rows = pl.ds(pl.multiple_of(step * 16, 16), 16)
            gate, lift, back = fw[s, 0, rows, :], fw[s, 1, rows, :], fw[s, 2, rows, :]
            g = jax.nn.sigmoid(gate)
            act = gate * g
            if s > 0:
                hb[s, 0, rows, :] = (act * lift).astype(BF)
            hb[s, 1, rows, :] = (back * lift * (g * (1.0 + gate * (1.0 - g)))).astype(BF)
            hb[s, 2, rows, :] = (back * act).astype(BF)
            gate, u, e = fw[s, 3, rows, :], fw[s, 4, rows, :], fw[s, 5, rows, :]
            g = jax.nn.sigmoid(gate)
            act = factor * gate * g
            slope = factor * (g * (1.0 + gate * (1.0 - g)))
            bend = factor * (g * (1.0 - g) * (2.0 + gate * (1.0 - 2.0 * g)))
            us = u * slope
            fw[s, 0, rows, :] = us
            fw[s, 1, rows, :] = e * u * bend
            fw[s, 2, rows, :] = e * slope
            fw[s, 3, rows, :] = act
            hb[s, 6, rows, :] = (act * u).astype(BF)
            hb[s, 7, rows, :] = (e * us).astype(BF)
            hb[s, 8, rows, :] = (e * act).astype(BF)

    def sides(s, b, m):
        ahead(qkv[s, 1] if m < 2 else qkv[s, 2], b, m, (s, (7, 8, 6)[m]))

    def second(s):
        @pl.loop(0, T // 16)
        def _(step):
            rows = pl.ds(pl.multiple_of(step * 16, 16), 16)
            pull, one, three = fw[s, 6, rows, :], fw[s, 7, rows, :], fw[s, 8, rows, :]
            us, eub, es, act = (fw[s, i, rows, :] for i in range(4))
            hb[s, 3, rows, :] = (us * pull + one * eub + three * es).astype(BF)
            hb[s, 4, rows, :] = (act * pull + one * es).astype(BF)
            hb[s, 5, rows, :] = (one * us + three * act).astype(BF)

    def back_queries(s, w):
        grad = behind(s, 1, w, 0) + behind(s, 2, w, 1)
        gcat[s, :, pl.ds(0, DH)] = grad.astype(BF)

    def back_sides(s, b):
        back[0] = behind(s, 7, b, 0) + behind(s, 8, b, 1)
        back[1] = behind(s, 6, b, 2)

    def back_rest(s, w):
        grad = behind(s, 3, w, 0) + behind(s, 4, w, 1) + back[0]
        gcat[s, :, pl.ds(DH, DH)] = grad.astype(BF)
        grad = behind(s, 5, w, 2) + back[1]
        gcat[s, :, pl.ds(2 * DH, DH)] = grad.astype(BF)

    pair = {}
    query_part, rest_part = pl.ds(0, DH), pl.ds(DH, 2 * DH)

    def exchange(s, i, lanes):
        pair[s, i] = send(
            gcat.at[s, :, lanes], gp.at[s, :, lanes], ps.at[s, i], pr_.at[s, i], dev(dc=1)
        )

    heads = {}
    steps = (2, 1, 3, 0)

    def own_term(s, step, lanes):
        rows = pl.multiple_of((lax.rem(x + step, NX) * 2 + c) * DH, DH)
        return mm_t(gcat[s, :, lanes], pc[pl.ds(rows, DH), lanes])

    def pair_term(s, step, lanes):
        return mm_t(gp[s, :, lanes], pp[lax.rem(x + step, NX), :, lanes])

    def heads_queries(s):
        pair[s, 0].wait_recv()
        for i, step in enumerate(steps):
            base[i] = own_term(s, step, query_part) + pair_term(s, step, query_part)

    def heads_send(s):
        for i, step in enumerate(steps):
            base[i] = base[i] + own_term(s, step, rest_part)
        pair[s, 1].wait_recv()
        heads[s] = []
        for i, step in enumerate(steps[:3]):
            pb[s, i] = (base[i] + pair_term(s, step, rest_part)).astype(BF)
            heads[s].append(
                send(pb.at[s, i], ro.at[s, i], hs.at[s, i], hr.at[s, i], dev(dx=step))
            )
        base[3] = base[3] + pair_term(s, 0, rest_part)

    def heads_end(s):
        total = base[3]
        for i in range(3):
            heads[s][i].wait_recv()
            total = total + ro[s, i].astype(F32)
        out[s] = total.astype(BF)

    far_end(0)
    assemble(W_LATE)
    gather_first(W_LATE)
    assemble(B_LATE)
    gather_first(B_LATE)
    gather_last(W_LATE)
    gather_last(B_LATE)
    x_relay(1)
    far_end(1)
    assemble(W_EARLY)
    gather_first(W_EARLY)
    project(1)
    for i, rows in enumerate((qkv[1, 1], qkv[1, 0], qkv[1, 2], o_s[1])):
        turned[i] = rows.T
    gather_end(W_LATE)
    forward(1, W_LATE)
    gather_end(B_LATE)
    for m in range(3):
        sides(1, B_LATE, m)
    second(1)

    terms = ((0, 3, 1, 1), (0, 4, 1, 2), (2, 5, 3, 0))
    sum_a, sum_b = {}, {}
    for m, (left, i, right, j) in enumerate(terms):
        for half in range(2):
            lanes = pl.ds(half * 256, 256)
            grad = mm(turned[left], hb[1, i, :, lanes]) + mm(turned[right], hb[1, j, :, lanes])
            grad = grad.reshape(4, 4, 16, 256)
            own[half, m] = grad
            rsend[half, m] = grad.astype(BF)
        sum_a[m] = [
            send(rsend.at[0, m, lax.rem(y + d, NY)], r1.at[0, m, n],
                 r1s.at[0, m, n], r1r.at[0, m, n], dev(dy=d))
            for n, d in enumerate((2, 1, 3))
        ]
        sum_b[m] = [
            send(rsend.at[1, m, :, lax.rem(z + d + NZ, 4)], r1.at[1, m, n],
                 r1s.at[1, m, n], r1r.at[1, m, n], dev(dz=d))
            for n, d in enumerate(near)
        ]

    back_queries(1, W_LATE)
    exchange(1, 0, query_part)
    back_sides(1, B_LATE)
    back_rest(1, W_LATE)
    exchange(1, 1, rest_part)

    for m in range(3):
        for copy in sum_a[m]:
            copy.wait_recv()
        total = own[0, m, y]
        for i in range(3):
            total = total + r1[0, m, i].astype(F32)
        acc[0, m] = total
        sd[0, m] = total.astype(BF)
    two_a = [
        send(sd.at[0, :, lax.rem(z + d + NZ, 4)], r2.at[0, n], r2s.at[0, n], r2r.at[0, n], dev(dz=d))
        for n, d in enumerate(near)
    ]
    for m in range(3):
        for copy in sum_b[m]:
            copy.wait_recv()
        total = own[1, m, :, zl]
        for i in range(3):
            total = total + r1[1, m, i].astype(F32)
        acc[1, m] = total
        sd[1, m] = total.astype(BF)
    two_b = [
        send(sd.at[1, :, lax.rem(y + d, NY)], r2.at[1, n], r2s.at[1, n], r2r.at[1, n], dev(dy=d))
        for n, d in enumerate((2, 1, 3))
    ]

    x_relay(0)
    loads[8].wait()
    project(0)

    flip = 4 - 8 * lax.rem(zh, 2)
    third = {}

    def far_sum(half, step):
        fsend[half, step] = part[half].astype(BF)
        way = flip if half == step else -flip
        third[half] = send(
            fsend.at[half, step], rf.at[half, step], rfs.at[half, step], rfr.at[half, step], dev(dz=way)
        )

    for half, copies, place in ((0, two_a, zl), (1, two_b, y)):
        for copy in copies:
            copy.wait_recv()
        total = acc[half, :, place]
        for i in range(3):
            total = total + r2[half, i].astype(F32)
        part[half] = total
        for k in range(4):
            mine = jnp.where(zh == k, 1.0, 0.0)
            for m in range(3):
                rows = pl.ds(4 * k, 4)
                part[half, m, rows, :] = (
                    part[half, m, rows, :] + mine * adjv[m, :, pl.ds(half * 256, 256)]
                )
        far_sum(half, 0)

    gather_last(W_EARLY)
    for half in range(2):
        third[half].wait_recv()
        part[half] = part[half] + rf[half, 0].astype(F32)
        far_sum(half, 1)
    for copy in pc_copies:
        copy.wait_recv()
    heads_queries(1)
    heads_send(1)
    for half in range(2):
        third[half].wait_recv()
        gath[B_EARLY, half, :, y, zl] = (part[half] + rf[half, 1].astype(F32)).astype(BF)
    gather_first(B_EARLY)
    gather_last(B_EARLY)
    gather_end(W_EARLY)
    forward(0, W_EARLY)
    back_queries(0, W_EARLY)
    exchange(0, 0, query_part)
    heads_end(1)
    heads_queries(0)
    gather_end(B_EARLY)

    for m in range(3):
        sides(0, B_EARLY, m)
    second(0)
    back_sides(0, B_EARLY)
    back_rest(0, W_EARLY)
    exchange(0, 1, rest_part)
    heads_send(0)
    heads_end(0)

    for copy in started:
        copy.wait_send()


def local(inputs, probe, address, payload, checkpoints, out_grad, adjoint, inner_rate):
    hbm = pl.BlockSpec(memory_space=pl.ANY)
    dma = pltpu.SemaphoreType.DMA
    scratch = [
        pltpu.VMEM((2, T, D), BF),
        pltpu.VMEM((3, D, DH), BF),
        pltpu.VMEM((D, 3 * DH), BF),
        pltpu.VMEM((4, DH, 3 * DH), BF),
        pltpu.VMEM((4, 2, 3, 4, 4, 16, 256), BF),
        pltpu.VMEM((3, 4, 3, 4, F), BF),
        pltpu.VMEM((3, 4, F), F32),
        pltpu.VMEM((3, 16, F), F32),
        pltpu.VMEM((2, T, DH), BF),
        pltpu.VMEM((2, 3, T, DH), BF),
        pltpu.VMEM((2, T, DH), BF),
        pltpu.VMEM((2, 9, T, F), F32),
        pltpu.VMEM((2, 9, T, F), BF),
        pltpu.VMEM((2, 3, 4, 4, 16, 256), F32),
        pltpu.VMEM((2, 3, 4, 4, 16, 256), BF),
        pltpu.VMEM((4, DH, T), BF),
        pltpu.VMEM((2, 3, 3, 4, 16, 256), BF),
        pltpu.VMEM((2, 3, 4, 16, 256), F32),
        pltpu.VMEM((2, 3, 4, 16, 256), BF),
        pltpu.VMEM((2, 3, 3, 16, 256), BF),
        pltpu.VMEM((2, 3, 16, 256), F32),
        pltpu.VMEM((2, 2, 3, 16, 256), BF),
        pltpu.VMEM((2, 2, 3, 16, 256), BF),
        pltpu.VMEM((2, T, 3 * DH), BF),
        pltpu.VMEM((2, T, 3 * DH), BF),
        pltpu.VMEM((2, T, DH), F32),
        pltpu.VMEM((4, T, DH), F32),
        pltpu.VMEM((2, 3, T, DH), BF),
        pltpu.VMEM((2, 3, T, DH), BF),
        dma((9,)),
    ]
    for shape in ((2, 7), (2, 4), (4, 2, 3), (4, 2, 3), (2, 3, 3), (2, 3), (2, 2), (4,), (2, 2), (2, 3)):
        scratch += [dma(shape), dma(shape)]
    return pl.pallas_call(
        kernel,
        name="meta_gradient",
        out_shape=jax.ShapeDtypeStruct((2, T, DH), BF),
        in_specs=[hbm] * 7 + [pl.BlockSpec(memory_space=pltpu.SMEM)],
        out_specs=pl.BlockSpec(memory_space=pltpu.VMEM),
        scratch_shapes=scratch,
        compiler_params=pltpu.CompilerParams(
            collective_id=0, has_side_effects=True, vmem_limit_bytes=60 * 2**20
        ),
    )(
        inputs,
        probe,
        address,
        payload,
        checkpoints.reshape(2, 3, 4, F),
        out_grad,
        adjoint.reshape(3, 4, F),
        inner_rate,
    )


def solution(mesh):
    split = Mesh(mesh.devices.reshape(NZ, NY, NX, NC), AXES)
    tok, head = ("z", "y"), ("x", "c")
    placed = (
        P(None, tok, head),
        P(None, head),
        P(None, head),
        P(None, head),
        P(None, None, head, tok, None),
        P(None, tok, head),
        P(None, head, tok, None),
        P(head),
    )
    return jax.shard_map(
        local, mesh=split, in_specs=placed, out_specs=P(None, tok, head), check_vma=False
    )
```
